32 devices in a mesh: section: 4 (over z), row: 2 (over x), col: 4 (over y, core).
Axes of the slice: x: 2, y: 2, z: 4, core: 2. Of those that a mesh axis runs over, the one named last changes fastest.
Arguments:
- input_fwd: bfloat16 [4, 256, 2560], P('section', 'col', 'row'), may hold values from -6 to 6
- input_bwd: bfloat16 [4, 256, 2560], P('section', 'col', 'row'), may hold values from -6 to 6
- cotangent: bfloat16 [4, 256, 2560], P('section', 'col', 'row'), may hold values from -0.375 to 0.375
- shared_up: bfloat16 [2560, 16384], P('row', ('col', 'section')), may hold values from -0.125 to 0.125
- shared_down: bfloat16 [16384, 2560], P(('col', 'section'), 'row'), may hold values from -0.046875 to 0.046875
- up_left: bfloat16 [4, 2560, 256], P('section', 'row'), may hold values from -0.125 to 0.125
- up_right: bfloat16 [4, 256, 16384], P('section', None, 'col'), may hold values from -0.1875 to 0.1875
- down_left: bfloat16 [4, 16384, 256], P('section', 'col'), may hold values from -0.046875 to 0.046875
- down_right: bfloat16 [4, 256, 2560], P('section', None, 'row'), may hold values from -0.1875 to 0.1875
Outputs:
- handoff_fwd: bfloat16 [4, 256, 2560], P('section', 'col', 'row')
- handoff_bwd: bfloat16 [4, 256, 2560], P('section', 'col', 'row')
- grad_shared_up: bfloat16 [2560, 16384], P('row', ('col', 'section'))
- grad_shared_down: bfloat16 [16384, 2560], P(('col', 'section'), 'row')
- grad_up_left: float32 [4, 2560, 256], P('section', 'row')
- grad_up_right: float32 [4, 256, 16384], P('section', None, 'col')
- grad_down_left: float32 [4, 16384, 256], P('section', 'col')
- grad_down_right: float32 [4, 256, 2560], P('section', None, 'row')
The draws below stay inside these ranges and needn't reach their ends.
All inputs are finite; a program needn't handle non-finite values.
Results may differ from the reference program's by a relative error of at most 0.022.
Values may be sent and summed in bfloat16 or wider, within the bound.
A program may use at most 128 MiB of HBM per device.

```python
import jax
import jax.numpy as jnp
from jax import lax

D = 2560
FF = 16384
R = 256
MICRO = 256
SECTIONS = 4


def shard_levels(stream_key, shape, shards, low, largest):
    factor_of, own = 1.0, jax.random.fold_in(stream_key, 6)
    for dim, blocks in shards:
        draws = jnp.exp(jax.random.uniform(jax.random.fold_in(own, dim), (blocks,), jnp.float32, low / len(shards), largest / len(shards)))
        factor_of = factor_of * jnp.repeat(draws, shape[dim] // blocks).reshape([-1 if axis == dim else 1 for axis in range(len(shape))])
    return factor_of


def centred(key, extent, scale, bound, cuts=(), dtype=jnp.bfloat16):
    drawn = jax.random.normal(key, extent, jnp.float32) * scale
    if len(cuts) > 0:
        drawn = shard_levels(key, extent, cuts, -0.22, 0.18) * drawn
    return jnp.clip(drawn, min=-bound, max=bound).astype(dtype)


def setup_inputs(seed: int = 0) -> dict:
    keys = jax.random.split(jax.random.key(seed), 10)
    return {
        "input_fwd": centred(keys[0], (SECTIONS, MICRO, D), 1.0, 6.0, ((0, 4), (1, 4), (2, 2))),
        "input_bwd": centred(keys[1], (SECTIONS, MICRO, D), 1.0, 6.0, ((0, 4), (1, 4), (2, 2))),
        "cotangent": centred(keys[2], (SECTIONS, MICRO, D), (MICRO ** -0.5), 0.375, ((0, 4), (1, 4), (2, 2))),
        "shared_up": centred(keys[3], (D, FF), D ** -0.5, 0.125, ((0, 2), (1, 16))),
        "shared_down": centred(keys[4], (FF, D), FF ** -0.5, 0.046875, ((0, 16), (1, 2))),
        "up_left": centred(keys[5], (SECTIONS, D, R), D ** -0.5, 0.125, ((0, 4), (1, 2))),
        "up_right": centred(keys[6], (SECTIONS, R, FF), (0.5 * R ** -0.5), 0.1875, ((0, 4), (2, 4))),
        "down_left": centred(keys[7], (SECTIONS, FF, R), FF ** -0.5, 0.046875, ((0, 4), (1, 4))),
        "down_right": centred(keys[8], (SECTIONS, R, D), (0.5 * R ** -0.5), 0.1875, ((0, 4), (2, 2))),
    }


def product(left, right):
    return jnp.dot(left, right, preferred_element_type=jnp.float32)


def silu_slope(preact):
    sigma = jax.nn.sigmoid(preact)
    return sigma * (1.0 + preact * (1.0 - sigma))


def one_section(shared_up, shared_down, section_data):
    input_fwd, input_bwd, cotangent, up_left, up_right, down_left, down_right = section_data
    count_fwd = input_fwd.shape[0]
    normed = jnp.concatenate([input_fwd, input_bwd], axis=0)
    delta_in = product(normed, up_left).astype(jnp.bfloat16)
    preact = product(normed, shared_up) + product(delta_in, up_right)
    hidden = jax.nn.silu(preact).astype(jnp.bfloat16)
    delta_out = product(hidden, down_left).astype(jnp.bfloat16)
    out_fwd = input_fwd.astype(jnp.float32) + product(hidden[:count_fwd], shared_down) + product(delta_out[:count_fwd], down_right)
    out_fwd = out_fwd.astype(jnp.bfloat16)
    hidden_bwd = hidden[count_fwd:]
    normed_bwd = normed[count_fwd:]
    din_bwd = delta_in[count_fwd:]
    dout_bwd = delta_out[count_fwd:]
    grad_down_right = product(dout_bwd.T, cotangent)
    grad_dout = product(cotangent, down_right.T).astype(jnp.bfloat16)
    grad_down_left = product(hidden_bwd.T, grad_dout)
    grad_hidden = product(cotangent, shared_down.T) + product(grad_dout, down_left.T)
    grad_preact = (grad_hidden * silu_slope(preact[count_fwd:])).astype(jnp.bfloat16)
    grad_up_right = product(din_bwd.T, grad_preact)
    grad_din = product(grad_preact, up_right.T).astype(jnp.bfloat16)
    grad_up_left = product(normed_bwd.T, grad_din)
    grad_normed = product(grad_preact, shared_up.T) + product(grad_din, up_left.T)
    grad_input = (cotangent.astype(jnp.float32) + grad_normed).astype(jnp.bfloat16)
    term_up = product(normed_bwd.T, grad_preact).astype(jnp.bfloat16).astype(jnp.float32)
    term_down = product(hidden_bwd.T, cotangent).astype(jnp.bfloat16).astype(jnp.float32)
    return out_fwd, grad_input, term_up, term_down, grad_up_left, grad_up_right, grad_down_left, grad_down_right


def reference(input_fwd, input_bwd, cotangent, shared_up, shared_down, up_left, up_right, down_left, down_right):
    def advance(totals, section_data):
        out_fwd, grad_input, term_up, term_down, g_ul, g_ur, g_dl, g_dr = one_section(shared_up, shared_down, section_data)
        totals = (totals[0] + term_up, totals[1] + term_down)
        return totals, (out_fwd, grad_input, g_ul, g_ur, g_dl, g_dr)

    start_totals = (jnp.zeros((D, FF), jnp.float32), jnp.zeros((FF, D), jnp.float32))
    totals, outputs = lax.scan(advance, start_totals, (input_fwd, input_bwd, cotangent, up_left, up_right, down_left, down_right))
    out_fwd, grad_input, g_ul, g_ur, g_dl, g_dr = outputs
    handoff_fwd = jnp.roll(out_fwd, 1, axis=0)
    handoff_bwd = jnp.roll(grad_input, -1, axis=0)
    grad_shared_up = totals[0].astype(jnp.bfloat16)
    grad_shared_down = totals[1].astype(jnp.bfloat16)
    return handoff_fwd, handoff_bwd, grad_shared_up, grad_shared_down, g_ul, g_ur, g_dl, g_dr
```

```python
import functools
import types

import jax
import jax.numpy as jnp
from jax import lax
from jax.experimental import pallas as pl
from jax.experimental.pallas import tpu as pltpu
from jax.sharding import PartitionSpec as P

F32, BF16 = jnp.float32, jnp.bfloat16


def from_behind(block, axis, distance):
    count = lax.axis_size(axis)
    return lax.ppermute(block, axis, [((i - distance) % count, i) for i in range(count)])


def row_sum(part):
    total = part.astype(F32)
    for step in range(1, lax.axis_size("row")):
        total = total + from_behind(part, "row", step).astype(F32)
    return total


def row_gather(block, axis):
    count, me = lax.axis_size("row"), lax.axis_index("row")
    wide = jnp.zeros(block.shape[:axis] + (count * block.shape[axis],) + block.shape[axis + 1 :], block.dtype)
    for step in range(count):
        piece = block if step == 0 else from_behind(block, "row", step)
        origin = (me - step) % count
        wide = lax.dynamic_update_slice_in_dim(wide, piece, origin * block.shape[axis], axis)
    return wide


def mm(spec, left, right):
    return jnp.einsum(spec, left, right, preferred_element_type=F32)


def silu_slope(preact):
    sigma = jax.nn.sigmoid(preact)
    return sigma * (1.0 + preact * (1.0 - sigma))


def local(
    input_fwd,
    input_bwd,
    cotangent,
    shared_up,
    shared_down,
    up_left,
    up_right,
    down_left,
    down_right,
):
    sections, rows = lax.axis_size("section"), lax.axis_size("row")
    section, row = lax.axis_index("section"), lax.axis_index("row")
    own, width = input_fwd.shape[1], input_fwd.shape[2]
    units = shared_up.shape[1]
    share = up_left.shape[2] // rows
    everyone = ("section", "col")
    micro = own * lax.axis_size("col")

    def own_share(block, axis):
        return lax.dynamic_slice_in_dim(block, row * share, share, axis)

    def own_section(tokens):
        return lax.dynamic_slice_in_dim(tokens, section * micro, micro, 0)

    def per_section(tokens):
        return tokens.reshape(sections, micro, tokens.shape[-1])

    x_fwd, x_bwd, cot = input_fwd[0], input_bwd[0], cotangent[0]
    all_bwd = lax.all_gather(x_bwd, everyone, axis=0, tiled=True)
    all_cot = lax.all_gather(cot, everyone, axis=0, tiled=True)
    all_fwd = lax.all_gather(x_fwd, everyone, axis=0, tiled=True)

    din_part = mm("tmd,dr->tmr", jnp.stack([x_fwd, x_bwd]), up_left[0])
    gdout_part = mm("md,rd->mr", cot, down_right[0])
    low_part = jnp.concatenate([din_part, gdout_part[None]]).astype(BF16)
    low = own_share(row_sum(low_part).astype(BF16), 2)
    low_all = lax.all_gather(low, everyone, axis=1, tiled=True)
    din_fwd, din_bwd, gdout = (per_section(low_all[i]) for i in range(3))

    right = lax.all_to_all(own_share(up_right[0], 0), "section", 1, 0, tiled=True)
    right = right.reshape(sections, share, units)
    left = lax.all_to_all(own_share(down_left[0], 0 + 1), "section", 0, 0, tiled=True)
    left = left.reshape(sections, units, share)

    def preact_of(tokens, din):
        part = mm("smd,df->smf", per_section(tokens), shared_up) + mm("smr,srf->smf", din, right)
        return row_sum(part.astype(BF16))

    pre_bwd = preact_of(all_bwd, din_bwd)
    ghid_part = mm("smd,fd->smf", per_section(all_cot), shared_down) + mm("smr,sfr->smf", gdout, left)
    grad_hidden = row_sum(ghid_part.astype(BF16))
    hid_bwd = jax.nn.silu(pre_bwd).astype(BF16)
    gpre = (grad_hidden * silu_slope(pre_bwd)).astype(BF16)
    flat_gpre = gpre.reshape(sections * micro, units)

    gnorm_part = mm("mf,df->md", flat_gpre, shared_up)
    gdin_part = mm("smf,srf->smr", gpre, right).reshape(sections * micro, share)
    back_part = jnp.concatenate([gnorm_part.astype(BF16), gdin_part.astype(BF16)], axis=1)
    back = lax.psum_scatter(back_part, everyone, scatter_dimension=0, tiled=True)
    gdin_own = row_gather(back[:, width:], 1)

    pre_fwd = preact_of(all_fwd, din_fwd)
    hid_fwd = jax.nn.silu(pre_fwd).astype(BF16)
    out_part = mm("mf,fd->md", hid_fwd.reshape(sections * micro, units), shared_down)
    dout_part = [
        mm("smf,sfr->smr", h, left).reshape(sections * micro, share).astype(BF16) for h in (hid_fwd, hid_bwd)
    ]
    ahead_part = jnp.concatenate([out_part.astype(BF16), *dout_part], axis=1)
    ahead = lax.psum_scatter(ahead_part, everyone, scatter_dimension=0, tiled=True)
    dout_own = row_gather(ahead[:, width:].reshape(own, 2, share), 2)

    grad_up = mm("md,mf->df", all_bwd, flat_gpre).astype(BF16)
    grad_down = mm("mf,md->fd", hid_bwd.reshape(sections * micro, units), all_cot).astype(BF16)

    grad_left = mm("smf,smr->sfr", hid_bwd, gdout).astype(BF16).reshape(sections * units, share)
    grad_left = lax.all_to_all(grad_left, "section", 0, 0, tiled=True)
    grad_down_left = row_gather(grad_left, 1).astype(F32)
    grad_right = mm("smr,smf->srf", din_bwd, gpre).astype(BF16).reshape(sections * share, units)
    grad_right = lax.all_to_all(grad_right, "section", 0, 1, tiled=True)
    grad_up_right = row_gather(grad_right, 0).astype(F32)

    grad_input = (
        cot.astype(F32) + back[:, :width].astype(F32) + mm("mr,dr->md", gdin_own, up_left[0])
    )
    handoff_bwd = from_behind(grad_input.astype(BF16)[None], "section", -1)
    gdin_all = lax.all_gather(gdin_own, "col", axis=0, tiled=True)
    grad_up_left = mm("md,mr->dr", own_section(all_bwd), gdin_all)

    out_fwd = (
        x_fwd.astype(F32) + ahead[:, :width].astype(F32) + mm("mr,rd->md", dout_own[:, 0], down_right[0])
    )
    handoff_fwd = from_behind(out_fwd.astype(BF16)[None], "section", 1)
    dout_all = lax.all_gather(dout_own[:, 1], "col", axis=0, tiled=True)
    grad_down_right = mm("mr,md->rd", dout_all, own_section(all_cot))
    return (
        handoff_fwd,
        handoff_bwd,
        grad_up,
        grad_down,
        grad_up_left[None],
        grad_up_right[None],
        grad_down_left[None],
        grad_down_right[None],
    )


MESH = pl.DeviceIdType.MESH
SECTION, ROW, COL = "section", "row", "col"
BWD, COT, FWD, LOW = range(4)
TILE = 256
FULL = 1
VMEM_BYTES = 63 * 1024 * 1024


def nn(left, right):
    return lax.dot_general(left, right, (((1,), (0,)), ((), ())), preferred_element_type=F32)


def nt(left, right):
    return lax.dot_general(left, right, (((1,), (1,)), ((), ())), preferred_element_type=F32)


def tn(left, right):
    return lax.dot_general(left, right, (((0,), (0,)), ((), ())), preferred_element_type=F32)


def at(index, size):
    return pl.ds(pl.multiple_of(index * size, size), size)


def scratch_of(S, C, own, width, units, rank):
    share, micro = rank // 2, own * C
    wide_b, wide_f = width + 2 * share, width + share
    arrays = dict(
        tok=(3, S, C, own, width),
        low=(S, C, 5, own, share),
        low_part=(3, own, rank),
        low_in=(3, own, rank),
        rt=(S, share, units),
        lt=(S, units, share),
        wu=(width, units),
        wd=(units, width),
        ul=(width, rank),
        dr=(rank, width),
        mine=(3, S, micro, units),
        theirs=(3, S, micro, units),
        rs_b=(S, 2, C // 2, own, wide_b),
        rk_b=(S, C // 2, own, wide_b),
        ry_b=(S, C // 2, own, wide_b),
        rs_f=(S, 2, C // 2, own, wide_f),
        rk_f=(S, C // 2, own, wide_f),
        ry_f=(S, C // 2, own, wide_f),
        zs_b=(S, own, wide_b),
        zr_b=(S, own, wide_b),
        zs_f=(S, own, wide_f),
        zr_f=(S, own, wide_f),
        gl_out=(S, 2, units, share),
        gr_out=(S, 2, share, units),
        gl_in=(2, S, units, share),
        gr_in=(2, S, share, units),
        gu_tile=(2, TILE, units),
        gd_tile=(2, TILE, width),
        rank_out=(3, own, share),
        rank_in=(3, own, share),
        rank_all=(C, 2, own, rank),
        hand=(2, own, width),
    )
    shapes = {name: pltpu.VMEM(shape, BF16) for name, shape in arrays.items()}
    shapes["gul"] = pltpu.VMEM((width, rank), F32)
    shapes["gdr"] = pltpu.VMEM((rank, width), F32)
    sems = dict(
        s_load=(12,),
        s_put=(6,),
        s_gput=(2, 2, S),
        s_gu_put=(2,),
        s_gd_put=(2,),
        s_tz=(2, 4, S),
        s_ty=(2, 4, S, C // 2),
        s_tk=(2, 4, S, C // 2),
        s_fac=(2, 2, S),
        s_low_x=(2,),
        s_pre=(2, 3, S),
        s_rk=(2, 2, S),
        s_ry=(2, 2, S, C // 2),
        s_rz=(2, 2, S),
        s_gz=(2, 4, S),
        s_gx=(2, 2, S),
        s_rank_x=(2, 2),
        s_rank_c=(2, C),
        s_hand_z=(2, 2),
    )
    for name, shape in sems.items():
        shapes[name] = pltpu.SemaphoreType.DMA(shape)
    return shapes


def vmem_need(shapes):
    total = 0
    for name, ref in shapes.items():
        if not name.startswith("s_"):
            size = jnp.dtype(ref.dtype).itemsize
            for extent in ref.shape:
                size *= extent
            total += size
    return total


def kernel(S, C, names, *refs):
    xf_h, xb_h, ct_h, wu_h, wd_h, ul_h, ur_h, dl_h, dr_h = refs[:9]
    hf_o, hb_o, gu_o, gd_o, gul_o, gl_o, gr_o, gdr_o = refs[9:17]
    v = types.SimpleNamespace(**dict(zip(names, refs[17:])))
    tok, low, rt, lt, mine, theirs = v.tok, v.low, v.rt, v.lt, v.mine, v.theirs
    wu, wd, ul, dr = v.wu, v.wd, v.ul, v.dr
    own, width = tok.shape[3], tok.shape[4]
    units, share = lt.shape[1], lt.shape[2]
    rank, micro, Y = 2 * share, own * C, C // 2
    z, r, c = (lax.axis_index(axis) for axis in (SECTION, ROW, COL))
    y, core = c // 2, lax.rem(c, 2)
    my_half, other_half = at(r, share), at(1 - r, share)

    def behind(d):
        return lax.rem(z - d + S, S)

    def ahead(d):
        return lax.rem(z + d, S)

    def col_up(e):
        return lax.rem(c + e, C)

    def col_down(e):
        return lax.rem(c - e + C, C)

    def y_up(g):
        return lax.rem(y + g, Y)

    def y_down(g):
        return lax.rem(y - g + Y, Y)

    def remote(source, target, sem, index, where):
        return pltpu.make_async_remote_copy(
            src_ref=source,
            dst_ref=target,
            send_sem=sem.at[(0,) + index],
            recv_sem=sem.at[(1,) + index],
            device_id=where,
            device_id_type=MESH,
        )

    def piece(t, s, col):
        return low.at[s, col] if t == LOW else tok.at[t, s, col]

    def tok_z(t, d):
        return remote(piece(t, z, c), piece(t, z, c), v.s_tz, (t, d), {SECTION: ahead(d)})

    def tok_z_in(t, d):
        here = piece(t, behind(d), c)
        return remote(here, here, v.s_tz, (t, d), {SECTION: ahead(d)})

    def tok_y(t, d, g):
        here = piece(t, behind(d), c)
        return remote(here, here, v.s_ty, (t, d, g), {COL: 2 * y_up(g) + core})

    def tok_y_in(t, d, g):
        here = piece(t, behind(d), 2 * y_down(g) + core)
        return remote(here, here, v.s_ty, (t, d, g), {COL: 2 * y_up(g) + core})

    def tok_k(t, d, g):
        here = piece(t, behind(d), 2 * y_down(g) + core)
        return remote(here, here, v.s_tk, (t, d, g), {COL: 2 * y + 1 - core})

    def tok_k_in(t, d, g):
        here = piece(t, behind(d), 2 * y_down(g) + 1 - core)
        return remote(here, here, v.s_tk, (t, d, g), {COL: 2 * y + 1 - core})

    def fac(k, d):
        if k == 0:
            return remote(ur_h.at[my_half, at(ahead(d), units)], rt.at[z], v.s_fac, (0, d), {SECTION: ahead(d)})
        return remote(dl_h.at[at(ahead(d), units), my_half], lt.at[z], v.s_fac, (1, d), {SECTION: ahead(d)})

    def fac_in(k, d):
        here = (rt if k == 0 else lt).at[behind(d)]
        return remote(here, here, v.s_fac, (k, d), {SECTION: ahead(d)})

    def low_x():
        return remote(v.low_part, v.low_in, v.s_low_x, (), {ROW: 1 - r})

    def pre(j, d):
        s = behind(d)
        return remote(mine.at[j, s], theirs.at[j, s], v.s_pre, (j, d), {ROW: 1 - r})

    def sums(j):
        return (v.rs_b, v.rk_b, v.ry_b, v.zs_b, v.zr_b) if j == 0 else (v.rs_f, v.rk_f, v.ry_f, v.zs_f, v.zr_f)

    def rs_k(j, d):
        rs, rk = sums(j)[:2]
        return remote(rs.at[behind(d), 1 - core], rk.at[behind(d)], v.s_rk, (j, d), {COL: 2 * y + 1 - core})

    def rs_y(j, d, g):
        rs, _, ry, _, _ = sums(j)
        s = behind(d)
        return remote(rs.at[s, core, y_up(g)], ry.at[s, y], v.s_ry, (j, d, g), {COL: 2 * y_up(g) + core})

    def rs_y_in(j, d, g):
        here = sums(j)[2].at[behind(d), y_down(g)]
        return remote(here, here, v.s_ry, (j, d, g), {COL: 2 * y_up(g) + core})

    def rs_z(j, d):
        zs, zr = sums(j)[3:]
        return remote(zs.at[behind(d)], zr.at[z], v.s_rz, (j, d), {SECTION: behind(d)})

    def rs_z_in(j, d):
        here = sums(j)[4].at[ahead(d)]
        return remote(here, here, v.s_rz, (j, d), {SECTION: behind(d)})

    def grad_slot(k, s, half):
        return (v.gl_in if k == 0 else v.gr_in).at[half, s]

    def grad_source(k, s, other):
        return (v.gl_out if k == 0 else v.gr_out).at[s, other]

    def halves(other):
        return 1 - r if other else r

    def grad_z(k, d, other=0):
        slot = grad_slot(k, z, halves(other))
        return remote(grad_source(k, behind(d), other), slot, v.s_gz, (2 * other + k, d), {SECTION: behind(d)})

    def grad_z_in(k, d, other=0):
        here = grad_slot(k, ahead(d), halves(other))
        return remote(here, here, v.s_gz, (2 * other + k, d), {SECTION: behind(d)})

    def grad_keep(k, other):
        source = grad_source(k, z, other)
        half = other_half if other else my_half
        target = gl_o.at[at(z, units), half] if k == 0 else gr_o.at[half, at(z, units)]
        return pltpu.make_async_copy(source, target, v.s_put.at[2 * other + k])

    def grad_put(k, d, half):
        s, lanes = ahead(d), pl.ds(half * share, share)
        target = gl_o.at[at(s, units), lanes] if k == 0 else gr_o.at[lanes, at(s, units)]
        return pltpu.make_async_copy(grad_slot(k, s, half), target, v.s_gput.at[k, half, d])

    def grad_x(k, d):
        here = grad_slot(k, ahead(d), r)
        return remote(here, here, v.s_gx, (k, d), {ROW: 1 - r})

    def grad_x_in(k, d):
        here = grad_slot(k, ahead(d), 1 - r)
        return remote(here, here, v.s_gx, (k, d), {ROW: 1 - r})

    def rank_x(j):
        block = pl.ds(0, 2) if j == 0 else pl.ds(2, 1)
        return remote(v.rank_out.at[block], v.rank_in.at[block], v.s_rank_x, (j,), {ROW: 1 - r})

    def rank_c(e):
        here = v.rank_all.at[c]
        return remote(here, here, v.s_rank_c, (e,), {COL: col_up(e)})

    def rank_c_in(e):
        here = v.rank_all.at[col_down(e)]
        return remote(here, here, v.s_rank_c, (e,), {COL: col_up(e)})

    def hand(j):
        if j == 0:
            return remote(v.hand.at[0], hb_o, v.s_hand_z, (0,), {SECTION: behind(1)})
        return remote(v.hand.at[1], hf_o, v.s_hand_z, (1,), {SECTION: ahead(1)})

    def spread(t, d):
        for g in range(1, Y):
            tok_y(t, d, g).start()
        tok_k(t, d, 0).start()

    def forward(t, d):
        tok_z_in(t, d).wait_recv()
        spread(t, d)

    def send(d):
        for t in (BWD, COT):
            tok_z(t, d).start()
        for k in range(2):
            fac(k, d).start()
        tok_z(FWD, d).start()

    def gathered(t, d):
        for g in range(1, Y):
            tok_y_in(t, d, g).wait_recv()
            tok_k(t, d, g).start()
        for g in range(Y):
            tok_k_in(t, d, g).wait_recv()

    def tokens(t, s):
        return tok[t, s].reshape(micro, width)

    def rank_tokens(t, s, half=r):
        return low[s, :, 4 if t == FWD else 2 * t + half].reshape(micro, share)

    def partial_up(j, t, d):
        s = behind(d)

        @pl.loop(0, units // min(TILE, units))
        def _(n):
            cols = at(n, min(TILE, units))
            part = nn(tokens(t, s), wu[:, cols]) + nn(rank_tokens(t, s), rt[s, :, cols])
            mine[j, s, :, cols] = part.astype(BF16)

        pre(j, d).start()

    def partial_down(d):
        s = behind(d)

        @pl.loop(0, units // min(TILE, units))
        def _(n):
            cols = at(n, min(TILE, units))
            part = nt(tokens(COT, s), wd[cols, :]) + nt(rank_tokens(COT, s), lt[s, cols, :])
            mine[1, s, :, cols] = part.astype(BF16)

        pre(1, d).start()

    def bwd_partials(d, first):
        gathered(BWD, d)
        gathered(LOW, d)
        if not first:
            fac_in(0, d).wait_recv()
        partial_up(0, BWD, d)
        gathered(COT, d)
        if not first:
            fac_in(1, d).wait_recv()
        partial_down(d)

    def fwd_partials(d):
        gathered(FWD, d)
        partial_up(2, FWD, d)

    def by_owner(rs, s, cols, part):
        part = part.astype(BF16)
        for col in range(C):
            rs[s, col % 2, col // 2, :, cols] = part[col * own : (col + 1) * own]

    def bwd_chunk(d):
        s = behind(d)
        for j in range(2):
            pre(j, d).wait()

        @pl.loop(0, units // min(TILE, units))
        def _(n):
            cols = at(n, min(TILE, units))
            p = mine[0, s, :, cols].astype(F32) + theirs[0, s, :, cols].astype(F32)
            g = mine[1, s, :, cols].astype(F32) + theirs[1, s, :, cols].astype(F32)
            sigma = jax.nn.sigmoid(p)
            mine[0, s, :, cols] = (p * sigma).astype(BF16)
            mine[1, s, :, cols] = (g * (sigma * (1.0 + p * (1.0 - sigma)))).astype(BF16)

        @pl.loop(0, width // TILE)
        def _(n):
            cols = at(n, TILE)
            by_owner(v.rs_b, s, cols, nt(mine[1, s], wu[cols, :]))

        by_owner(v.rs_b, s, slice(width, width + share), nt(mine[1, s], rt[s]))
        by_owner(v.rs_b, s, slice(width + share, width + 2 * share), nn(mine[0, s], lt[s]))
        rs_k(0, d).start()
        v.gl_out[s, 0] = tn(mine[0, s], rank_tokens(COT, s)).astype(BF16)
        v.gr_out[s, 0] = tn(rank_tokens(BWD, s), mine[1, s]).astype(BF16)

        @pl.when(d > 0)
        def _():
            for k in range(2):
                grad_z(k, d).start()

        @pl.when(d < FULL)
        def _():
            v.gl_out[s, 1] = tn(mine[0, s], rank_tokens(COT, s, 1 - r)).astype(BF16)
            v.gr_out[s, 1] = tn(rank_tokens(BWD, s, 1 - r), mine[1, s]).astype(BF16)

        @pl.when((d < FULL) & (d > 0))
        def _():
            for k in range(2):
                grad_z(k, d, 1).start()

        @pl.when(d == 0)
        def _():
            for k in range(2):
                for other in range(2):
                    grad_keep(k, other).start()

    def fwd_chunk(d):
        s = behind(d)
        pre(2, d).wait()

        @pl.loop(0, units // min(TILE, units))
        def _(n):
            cols = at(n, min(TILE, units))
            p = mine[2, s, :, cols].astype(F32) + theirs[2, s, :, cols].astype(F32)
            mine[2, s, :, cols] = (p * jax.nn.sigmoid(p)).astype(BF16)

        @pl.loop(0, width // TILE)
        def _(n):
            cols = at(n, TILE)
            by_owner(v.rs_f, s, cols, nn(mine[2, s], wd[:, cols]))

        by_owner(v.rs_f, s, slice(width, width + share), nn(mine[2, s], lt[s]))
        rs_k(1, d).start()

    def reduce_core(j, d):
        s = behind(d)
        rs, rk = sums(j)[:2]
        rs_k(j, d).wait()
        rs[s, core] = (rs[s, core].astype(F32) + rk[s].astype(F32)).astype(BF16)
        for g in range(1, Y):
            rs_y(j, d, g).start()

    def reduce_chunk(j, d):
        s = behind(d)
        rs, _, ry, zs, zr = sums(j)
        total = rs[s, core, y].astype(F32)
        for g in range(1, Y):
            rs_y_in(j, d, g).wait_recv()
            total = total + ry[s, y_down(g)].astype(F32)

        @pl.when(d == 0)
        def _():
            zr[z] = total.astype(BF16)

        @pl.when(d > 0)
        def _():
            zs[s] = total.astype(BF16)
            rs_z(j, d).start()

    def pass_on(d):
        for k in range(2):
            grad_z_in(k, d).wait_recv()
            grad_x(k, d).start()

    def home_sum(j):
        zr = sums(j)[4]
        for d in range(1, S):
            rs_z_in(j, d).wait_recv()
        total = zr[0].astype(F32)
        for s in range(1, S):
            total = total + zr[s].astype(F32)
        return total

    def grad_up():
        step = min(TILE, units)

        @pl.loop(0, width // TILE)
        def _(m):
            slot = lax.rem(m, 2)
            put = pltpu.make_async_copy(v.gu_tile.at[slot], gu_o.at[at(m, TILE), :], v.s_gu_put.at[slot])

            @pl.when(m >= 2)
            def _():
                put.wait()

            for n in range(units // step):
                left = tok[BWD, :, :, :, at(m, TILE)].reshape(S * micro, TILE)
                right = mine[1, :, :, n * step : (n + 1) * step].reshape(S * micro, step)
                v.gu_tile[slot, :, n * step : (n + 1) * step] = tn(left, right).astype(BF16)
            put.start()

    def grad_down():
        tall = min(TILE, units)

        @pl.loop(0, units // tall)
        def _(m):
            slot = lax.rem(m, 2)
            put = pltpu.make_async_copy(
                v.gd_tile.at[slot, :tall], gd_o.at[at(m, tall), :], v.s_gd_put.at[slot]
            )

            @pl.when(m >= 2)
            def _():
                put.wait()

            for n in range(width // TILE):
                left = mine[0, :, :, at(m, tall)].reshape(S * micro, tall)
                right = tok[COT, :, :, :, n * TILE : (n + 1) * TILE].reshape(S * micro, TILE)
                v.gd_tile[slot, :tall, n * TILE : (n + 1) * TILE] = tn(left, right).astype(BF16)
            put.start()

    def drain_tiles(sem, tile, out, tall, count):
        for m in range(max(0, count - 2), count):
            pltpu.make_async_copy(
                tile.at[m % 2, :tall], out.at[m * tall : (m + 1) * tall, :], sem.at[m % 2]
            ).wait()

    loads = [
        (xb_h, tok.at[BWD, z, c]),
        (ct_h, tok.at[COT, z, c]),
        (xf_h, tok.at[FWD, z, c]),
        (ul_h, ul),
        (dr_h, dr),
        (wu_h, wu),
        (ur_h.at[my_half, at(z, units)], rt.at[z]),
        (wd_h, wd),
        (dl_h.at[at(z, units), my_half], lt.at[z]),
    ]
    loads = [pltpu.make_async_copy(a, b, v.s_load.at[i]) for i, (a, b) in enumerate(loads)]
    for copy in loads:
        copy.start()
    barrier = pltpu.get_barrier_semaphore()
    pl.semaphore_signal(barrier, inc=1, device_id={ROW: 1 - r}, device_id_type=MESH)
    for e in range(1, C):
        pl.semaphore_signal(barrier, inc=1, device_id={COL: col_up(e)}, device_id_type=MESH)
    for d in range(1, S):
        pl.semaphore_signal(barrier, inc=1, device_id={SECTION: ahead(d)}, device_id_type=MESH)
    for copy in loads[:3]:
        copy.wait()
    pl.semaphore_wait(barrier, S + C - 1)

    spread(BWD, 0)
    spread(COT, 0)
    send(1)
    for copy in loads[3:5]:
        copy.wait()
    v.low_part[BWD] = nn(tok[BWD, z, c], ul[...]).astype(BF16)
    v.low_part[COT] = nt(tok[COT, z, c], dr[...]).astype(BF16)
    v.low_part[FWD] = nn(tok[FWD, z, c], ul[...]).astype(BF16)
    low_x().start()
    low_x().wait()
    for t in (BWD, COT):
        for half in range(2):
            cols = pl.ds(half * share, share)
            low[z, c, 2 * t + half] = (v.low_part[t, :, cols].astype(F32) + v.low_in[t, :, cols].astype(F32)).astype(BF16)
    low[z, c, 4] = (v.low_part[FWD, :, my_half].astype(F32) + v.low_in[FWD, :, my_half].astype(F32)).astype(BF16)
    spread(LOW, 0)
    for d in range(1, S):
        tok_z(LOW, d).start()
    spread(FWD, 0)
    for copy in loads[5:]:
        copy.wait()
    bwd_partials(0, True)
    fwd_partials(0)
    for t in (BWD, LOW, COT, FWD):
        forward(t, 1)
    send(2)

    @pl.loop(0, S)
    def _(i):
        @pl.when(i + 1 < S)
        def _():
            bwd_partials(i + 1, False)
            fwd_partials(i + 1)

        @pl.when(i > 0)
        def _():
            reduce_chunk(0, i - 1)
            reduce_chunk(1, i - 1)

        bwd_chunk(i)
        reduce_core(0, i)
        fwd_chunk(i)
        reduce_core(1, i)

        @pl.when(i + 2 < S)
        def _():
            for t in (BWD, LOW, COT, FWD):
                forward(t, i + 2)

        @pl.when(i + 3 < S)
        def _():
            send(i + 3)

        @pl.when(i > FULL)
        def _():
            pass_on(i - 1)

    reduce_chunk(0, S - 1)
    reduce_chunk(1, S - 1)
    grad_up()
    if FULL < S:
        pass_on(S - 1)

    total = home_sum(0)
    v.rank_out[0] = total[:, width : width + share].astype(BF16)
    v.rank_out[1] = total[:, width + share :].astype(BF16)
    rank_x(0).start()
    grad_norm = total[:, :width] + tok[COT, z, c].astype(F32)
    rank_x(0).wait()
    v.rank_all[c, :, :, my_half] = v.rank_out[0:2]
    v.rank_all[c, :, :, other_half] = v.rank_in[0:2]
    for e in range(1, C):
        rank_c(e).start()
    v.hand[0] = (grad_norm + nt(v.rank_all[c, 0], ul[...])).astype(BF16)
    hand(0).start()

    grad_down()

    total = home_sum(1)
    v.rank_out[2] = total[:, width:].astype(BF16)
    rank_x(1).start()
    for e in range(1, C):
        rank_c_in(e).wait_recv()
    v.gul[...] = tn(tokens(BWD, z), v.rank_all[:, 0].reshape(micro, rank))
    put_up = pltpu.make_async_copy(v.gul, gul_o, v.s_put.at[4])
    put_up.start()
    v.gdr[...] = tn(v.rank_all[:, 1].reshape(micro, rank), tokens(COT, z))
    put_down = pltpu.make_async_copy(v.gdr, gdr_o, v.s_put.at[5])
    put_down.start()
    rank_x(1).wait()
    out = total[:, :width] + tok[FWD, z, c].astype(F32)
    out = out + nn(v.rank_out[2], dr[my_half, :]) + nn(v.rank_in[2], dr[other_half, :])
    v.hand[1] = out.astype(BF16)
    hand(1).start()

    for k in range(2):
        for other in range(2):
            grad_keep(k, other).wait()
        for d in range(1, FULL):
            grad_z_in(k, d).wait_recv()
            grad_z_in(k, d, 1).wait_recv()
            grad_z(k, d, 1).wait_send()
            for half in range(2):
                grad_put(k, d, half).start()

    @pl.loop(FULL, S)
    def _(d):
        for k in range(2):
            grad_x(k, d).wait_send()
            grad_x_in(k, d).wait_recv()
            for half in range(2):
                grad_put(k, d, half).start()

    tall = min(TILE, units)
    drain_tiles(v.s_gu_put, v.gu_tile, gu_o, TILE, width // TILE)
    drain_tiles(v.s_gd_put, v.gd_tile, gd_o, tall, units // tall)
    put_up.wait()
    put_down.wait()

    @pl.loop(1, S)
    def _(d):
        for t in range(4):
            tok_z(t, d).wait_send()
        for k in range(2):
            fac(k, d).wait_send()
            grad_z(k, d).wait_send()
            rs_z(k, d).wait_send()

    @pl.loop(0, S)
    def _(d):
        for t in range(4):
            for g in range(Y):
                tok_k(t, d, g).wait_send()
            for g in range(1, Y):
                tok_y(t, d, g).wait_send()
        for j in range(2):
            for g in range(1, Y):
                rs_y(j, d, g).wait_send()

    for e in range(1, C):
        rank_c(e).wait_send()
    for j in range(2):
        hand(j).wait()

    @pl.loop(1, S)
    def _(d):
        for k in range(2):
            for half in range(2):
                grad_put(k, d, half).wait()


def finish_kernel(count, *refs):
    ins, outs, near, wide = refs[:8], refs[8:16], refs[16:24], refs[24:26]
    s_in, s_out = refs[26:]
    pieces = []
    for i in (5, 6, 2, 3, 4, 7, 0, 1):
        parts = count if i in (2, 3, 5, 6) else 1
        tall = ins[i].shape[0] // parts
        for p in range(parts):
            rows = pl.ds(p * tall, tall)
            final = wide[i - 5] if i in (5, 6) else near[i]
            load = pltpu.make_async_copy(ins[i].at[rows], near[i].at[rows], s_in.at[i, p])
            store = pltpu.make_async_copy(final.at[rows], outs[i].at[rows], s_out.at[i, p])
            pieces.append((i, rows, load, store))
    for _, _, load, _ in pieces:
        load.start()
    for i, rows, load, store in pieces:
        load.wait()
        if i in (5, 6):
            wide[i - 5][rows] = near[i][rows].astype(F32)
        store.start()
    for _, _, _, store in pieces:
        store.wait()


def finish(arrays):
    whole, count = pl.BlockSpec(memory_space=pl.ANY), 4
    outs = [jax.ShapeDtypeStruct(a.shape, F32 if i in (5, 6) else a.dtype) for i, a in enumerate(arrays)]
    return pl.pallas_call(
        functools.partial(finish_kernel, count),
        out_shape=outs,
        in_specs=[whole] * len(outs),
        out_specs=[whole] * len(outs),
        scratch_shapes=[pltpu.VMEM(a.shape, a.dtype) for a in arrays]
        + [pltpu.VMEM(outs[i].shape, F32) for i in (5, 6)]
        + [pltpu.SemaphoreType.DMA((8, count))] * 2,
        compiler_params=pltpu.CompilerParams(vmem_limit_bytes=VMEM_BYTES),
    )(*arrays)


def fused(*args):
    S, C = lax.axis_size(SECTION), lax.axis_size(COL)
    own, width = args[0].shape[1:]
    units, rank = args[3].shape[1], args[5].shape[2]
    shapes = scratch_of(S, C, own, width, units, rank)
    outs = [
        ((own, width), BF16),
        ((own, width), BF16),
        ((width, units), BF16),
        ((units, width), BF16),
        ((width, rank), F32),
        ((S * units, rank), BF16),
        ((rank, S * units), BF16),
        ((rank, width), F32),
    ]
    whole = pl.BlockSpec(memory_space=pl.ANY)
    tokens = 3 * S * own * C
    outputs = pl.pallas_call(
        functools.partial(kernel, S, C, list(shapes)),
        out_shape=[jax.ShapeDtypeStruct(*out) for out in outs],
        in_specs=[whole] * len(args),
        out_specs=[whole] * len(outs),
        scratch_shapes=list(shapes.values()),
        compiler_params=pltpu.CompilerParams(
            collective_id=0, has_side_effects=True, vmem_limit_bytes=VMEM_BYTES
        ),
        cost_estimate=pl.CostEstimate(
            flops=6 * tokens * width * units, bytes_accessed=20 * width * units, transcendentals=tokens * units
        ),
    )(*[arg[0] if arg.ndim == 3 else arg for arg in args])
    hand_f, hand_b, grad_up, grad_down, grad_ul, grad_dl, grad_ur, grad_dr = finish(outputs)
    return (
        hand_f[None],
        hand_b[None],
        grad_up,
        grad_down,
        grad_ul[None],
        grad_ur[None],
        grad_dl[None],
        grad_dr[None],
    )


def step(*args):
    S, C, rows = (lax.axis_size(axis) for axis in (SECTION, COL, ROW))
    own, width = args[0].shape[1:]
    units, rank = args[3].shape[1], args[5].shape[2]
    shapes = scratch_of(S, C, own, width, units, rank)
    fits = vmem_need(shapes) <= VMEM_BYTES - (2 << 20)
    even = rows == 2 and S > 2 and C % 2 == 0 and width % TILE == 0 and (units % TILE == 0 or units == 128)
    if fits and even and rank == 256 and own % 16 == 0:
        return fused(*args)
    return local(*args)


def solution(mesh):
    in_specs = (
        P("section", "col", "row"),
        P("section", "col", "row"),
        P("section", "col", "row"),
        P("row", ("col", "section")),
        P(("col", "section"), "row"),
        P("section", "row", None),
        P("section", None, "col"),
        P("section", "col", None),
        P("section", None, "row"),
    )
    out_specs = (
        P("section", "col", "row"),
        P("section", "col", "row"),
        P("row", ("col", "section")),
        P(("col", "section"), "row"),
        P("section", "row", None),
        P("section", None, "col"),
        P("section", "col", None),
        P("section", None, "row"),
    )
    return jax.shard_map(step, mesh=mesh, in_specs=in_specs, out_specs=out_specs, check_vma=False)
```

```python
import functools
import types

import jax
import jax.numpy as jnp
from jax import lax
from jax.experimental import pallas as pl
from jax.experimental.pallas import tpu as pltpu
from jax.sharding import PartitionSpec as P

F32, BF16 = jnp.float32, jnp.bfloat16


def from_behind(block, axis, distance):
    count = lax.axis_size(axis)
    return lax.ppermute(block, axis, [((i - distance) % count, i) for i in range(count)])


def row_sum(part):
    total = part.astype(F32)
    for step in range(1, lax.axis_size("row")):
        total = total + from_behind(part, "row", step).astype(F32)
    return total


def row_gather(block, axis):
    count, me = lax.axis_size("row"), lax.axis_index("row")
    wide = jnp.zeros(block.shape[:axis] + (count * block.shape[axis],) + block.shape[axis + 1 :], block.dtype)
    for step in range(count):
        piece = block if step == 0 else from_behind(block, "row", step)
        origin = (me - step) % count
        wide = lax.dynamic_update_slice_in_dim(wide, piece, origin * block.shape[axis], axis)
    return wide


def mm(spec, left, right):
    return jnp.einsum(spec, left, right, preferred_element_type=F32)


def silu_slope(preact):
    sigma = jax.nn.sigmoid(preact)
    return sigma * (1.0 + preact * (1.0 - sigma))


def local(
    input_fwd,
    input_bwd,
    cotangent,
    shared_up,
    shared_down,
    up_left,
    up_right,
    down_left,
    down_right,
):
    sections, rows = lax.axis_size("section"), lax.axis_size("row")
    section, row = lax.axis_index("section"), lax.axis_index("row")
    own, width = input_fwd.shape[1], input_fwd.shape[2]
    units = shared_up.shape[1]
    share = up_left.shape[2] // rows
    everyone = ("section", "col")
    micro = own * lax.axis_size("col")

    def own_share(block, axis):
        return lax.dynamic_slice_in_dim(block, row * share, share, axis)

    def own_section(tokens):
        return lax.dynamic_slice_in_dim(tokens, section * micro, micro, 0)

    def per_section(tokens):
        return tokens.reshape(sections, micro, tokens.shape[-1])

    x_fwd, x_bwd, cot = input_fwd[0], input_bwd[0], cotangent[0]
    all_bwd = lax.all_gather(x_bwd, everyone, axis=0, tiled=True)
    all_cot = lax.all_gather(cot, everyone, axis=0, tiled=True)
    all_fwd = lax.all_gather(x_fwd, everyone, axis=0, tiled=True)

    din_part = mm("tmd,dr->tmr", jnp.stack([x_fwd, x_bwd]), up_left[0])
    gdout_part = mm("md,rd->mr", cot, down_right[0])
    low_part = jnp.concatenate([din_part, gdout_part[None]]).astype(BF16)
    low = own_share(row_sum(low_part).astype(BF16), 2)
    low_all = lax.all_gather(low, everyone, axis=1, tiled=True)
    din_fwd, din_bwd, gdout = (per_section(low_all[i]) for i in range(3))

    right = lax.all_to_all(own_share(up_right[0], 0), "section", 1, 0, tiled=True)
    right = right.reshape(sections, share, units)
    left = lax.all_to_all(own_share(down_left[0], 0 + 1), "section", 0, 0, tiled=True)
    left = left.reshape(sections, units, share)

    def preact_of(tokens, din):
        part = mm("smd,df->smf", per_section(tokens), shared_up) + mm("smr,srf->smf", din, right)
        return row_sum(part.astype(BF16))

    pre_bwd = preact_of(all_bwd, din_bwd)
    ghid_part = mm("smd,fd->smf", per_section(all_cot), shared_down) + mm("smr,sfr->smf", gdout, left)
    grad_hidden = row_sum(ghid_part.astype(BF16))
    hid_bwd = jax.nn.silu(pre_bwd).astype(BF16)
    gpre = (grad_hidden * silu_slope(pre_bwd)).astype(BF16)
    flat_gpre = gpre.reshape(sections * micro, units)

    gnorm_part = mm("mf,df->md", flat_gpre, shared_up)
    gdin_part = mm("smf,srf->smr", gpre, right).reshape(sections * micro, share)
    back_part = jnp.concatenate([gnorm_part.astype(BF16), gdin_part.astype(BF16)], axis=1)
    back = lax.psum_scatter(back_part, everyone, scatter_dimension=0, tiled=True)
    gdin_own = row_gather(back[:, width:], 1)

    pre_fwd = preact_of(all_fwd, din_fwd)
    hid_fwd = jax.nn.silu(pre_fwd).astype(BF16)
    out_part = mm("mf,fd->md", hid_fwd.reshape(sections * micro, units), shared_down)
    dout_part = [
        mm("smf,sfr->smr", h, left).reshape(sections * micro, share).astype(BF16) for h in (hid_fwd, hid_bwd)
    ]
    ahead_part = jnp.concatenate([out_part.astype(BF16), *dout_part], axis=1)
    ahead = lax.psum_scatter(ahead_part, everyone, scatter_dimension=0, tiled=True)
    dout_own = row_gather(ahead[:, width:].reshape(own, 2, share), 2)

    grad_up = mm("md,mf->df", all_bwd, flat_gpre).astype(BF16)
    grad_down = mm("mf,md->fd", hid_bwd.reshape(sections * micro, units), all_cot).astype(BF16)

    grad_left = mm("smf,smr->sfr", hid_bwd, gdout).astype(BF16).reshape(sections * units, share)
    grad_left = lax.all_to_all(grad_left, "section", 0, 0, tiled=True)
    grad_down_left = row_gather(grad_left, 1).astype(F32)
    grad_right = mm("smr,smf->srf", din_bwd, gpre).astype(BF16).reshape(sections * share, units)
    grad_right = lax.all_to_all(grad_right, "section", 0, 1, tiled=True)
    grad_up_right = row_gather(grad_right, 0).astype(F32)

    grad_input = (
        cot.astype(F32) + back[:, :width].astype(F32) + mm("mr,dr->md", gdin_own, up_left[0])
    )
    handoff_bwd = from_behind(grad_input.astype(BF16)[None], "section", -1)
    gdin_all = lax.all_gather(gdin_own, "col", axis=0, tiled=True)
    grad_up_left = mm("md,mr->dr", own_section(all_bwd), gdin_all)

    out_fwd = (
        x_fwd.astype(F32) + ahead[:, :width].astype(F32) + mm("mr,rd->md", dout_own[:, 0], down_right[0])
    )
    handoff_fwd = from_behind(out_fwd.astype(BF16)[None], "section", 1)
    dout_all = lax.all_gather(dout_own[:, 1], "col", axis=0, tiled=True)
    grad_down_right = mm("mr,md->rd", dout_all, own_section(all_cot))
    return (
        handoff_fwd,
        handoff_bwd,
        grad_up,
        grad_down,
        grad_up_left[None],
        grad_up_right[None],
        grad_down_left[None],
        grad_down_right[None],
    )


MESH = pl.DeviceIdType.MESH
SECTION, ROW, COL = "section", "row", "col"
BWD, COT, FWD, LOW = range(4)
TILE = 256
FULL = 1
VMEM_BYTES = 63 * 1024 * 1024


def nn(left, right):
    return lax.dot_general(left, right, (((1,), (0,)), ((), ())), preferred_element_type=F32)


def nt(left, right):
    return lax.dot_general(left, right, (((1,), (1,)), ((), ())), preferred_element_type=F32)


def tn(left, right):
    return lax.dot_general(left, right, (((0,), (0,)), ((), ())), preferred_element_type=F32)


def at(index, size):
    return pl.ds(pl.multiple_of(index * size, size), size)


def scratch_of(S, C, own, width, units, rank):
    share, micro = rank // 2, own * C
    wide_b, wide_f = width + 2 * share, width + share
    arrays = dict(
        tok=(3, S, C, own, width),
        low=(S, C, 5, own, share),
        low_part=(3, own, rank),
        low_in=(3, own, rank),
        rt=(S, share, units),
        lt=(S, units, share),
        wu=(width, units),
        wd=(units, width),
        ul=(width, rank),
        dr=(rank, width),
        mine=(3, S, micro, units),
        theirs=(3, S, micro, units),
        rs_b=(S, 2, C // 2, own, wide_b),
        rk_b=(S, C // 2, own, wide_b),
        ry_b=(S, C // 2, own, wide_b),
        rs_f=(S, 2, C // 2, own, wide_f),
        rk_f=(S, C // 2, own, wide_f),
        ry_f=(S, C // 2, own, wide_f),
        zs_b=(S, own, wide_b),
        zr_b=(S, own, wide_b),
        zs_f=(S, own, wide_f),
        zr_f=(S, own, wide_f),
        gl_out=(S, 2, units, share),
        gr_out=(S, 2, share, units),
        gl_in=(2, S, units, share),
        gr_in=(2, S, share, units),
        gu_tile=(2, TILE, units),
        gd_tile=(2, TILE, width),
        rank_out=(3, own, share),
        rank_in=(3, own, share),
        rank_all=(C, 2, own, rank),
        hand=(2, own, width),
    )
    shapes = {name: pltpu.VMEM(shape, BF16) for name, shape in arrays.items()}
    shapes["gul"] = pltpu.VMEM((width, rank), F32)
    shapes["gdr"] = pltpu.VMEM((rank, width), F32)
    sems = dict(
        s_load=(12,),
        s_put=(6,),
        s_gput=(2, 2, S),
        s_gu_put=(2,),
        s_gd_put=(2,),
        s_tz=(2, 4, S),
        s_ty=(2, 4, S, C // 2),
        s_tk=(2, 4, S, C // 2),
        s_fac=(2, 2, S),
        s_low_x=(2,),
        s_pre=(2, 3, S),
        s_rk=(2, 2, S),
        s_ry=(2, 2, S, C // 2),
        s_rz=(2, 2, S),
        s_gz=(2, 4, S),
        s_gx=(2, 2, S),
        s_rank_x=(2, 2),
        s_rank_c=(2, C),
        s_hand_z=(2, 2),
    )
    for name, shape in sems.items():
        shapes[name] = pltpu.SemaphoreType.DMA(shape)
    return shapes


def vmem_need(shapes):
    total = 0
    for name, ref in shapes.items():
        if not name.startswith("s_"):
            size = jnp.dtype(ref.dtype).itemsize
            for extent in ref.shape:
                size *= extent
            total += size
    return total


def kernel(S, C, names, *refs):
    xf_h, xb_h, ct_h, wu_h, wd_h, ul_h, ur_h, dl_h, dr_h = refs[:9]
    hf_o, hb_o, gu_o, gd_o, gul_o, gl_o, gr_o, gdr_o = refs[9:17]
    v = types.SimpleNamespace(**dict(zip(names, refs[17:])))
    tok, low, rt, lt, mine, theirs = v.tok, v.low, v.rt, v.lt, v.mine, v.theirs
    wu, wd, ul, dr = v.wu, v.wd, v.ul, v.dr
    own, width = tok.shape[3], tok.shape[4]
    units, share = lt.shape[1], lt.shape[2]
    rank, micro, Y = 2 * share, own * C, C // 2
    z, r, c = (lax.axis_index(axis) for axis in (SECTION, ROW, COL))
    y, core = c // 2, lax.rem(c, 2)
    my_half, other_half = at(r, share), at(1 - r, share)

    def behind(d):
        return lax.rem(z - d + S, S)

    def ahead(d):
        return lax.rem(z + d, S)

    def col_up(e):
        return lax.rem(c + e, C)

    def col_down(e):
        return lax.rem(c - e + C, C)

    def y_up(g):
        return lax.rem(y + g, Y)

    def y_down(g):
        return lax.rem(y - g + Y, Y)

    def remote(source, target, sem, index, where):
        return pltpu.make_async_remote_copy(
            src_ref=source,
            dst_ref=target,
            send_sem=sem.at[(0,) + index],
            recv_sem=sem.at[(1,) + index],
            device_id=where,
            device_id_type=MESH,
        )

    def piece(t, s, col):
        return low.at[s, col] if t == LOW else tok.at[t, s, col]

    def tok_z(t, d):
        here = piece(t, behind(d - 1), c)
        return remote(here, here, v.s_tz, (t, d), {SECTION: ahead(1)})

    def tok_z_in(t, d):
        here = piece(t, behind(d), c)
        return remote(here, here, v.s_tz, (t, d), {SECTION: ahead(1)})

    def tok_y(t, d, g):
        here = piece(t, behind(d), c)
        return remote(here, here, v.s_ty, (t, d, g), {COL: 2 * y_up(g) + core})

    def tok_y_in(t, d, g):
        here = piece(t, behind(d), 2 * y_down(g) + core)
        return remote(here, here, v.s_ty, (t, d, g), {COL: 2 * y_up(g) + core})

    def tok_k(t, d, g):
        here = piece(t, behind(d), 2 * y_down(g) + core)
        return remote(here, here, v.s_tk, (t, d, g), {COL: 2 * y + 1 - core})

    def tok_k_in(t, d, g):
        here = piece(t, behind(d), 2 * y_down(g) + 1 - core)
        return remote(here, here, v.s_tk, (t, d, g), {COL: 2 * y + 1 - core})

    def fac(k, d):
        if k == 0:
            return remote(ur_h.at[my_half, at(ahead(d), units)], rt.at[z], v.s_fac, (0, d), {SECTION: ahead(d)})
        return remote(dl_h.at[at(ahead(d), units), my_half], lt.at[z], v.s_fac, (1, d), {SECTION: ahead(d)})

    def fac_in(k, d):
        here = (rt if k == 0 else lt).at[behind(d)]
        return remote(here, here, v.s_fac, (k, d), {SECTION: ahead(d)})

    def low_x():
        return remote(v.low_part, v.low_in, v.s_low_x, (), {ROW: 1 - r})

    def pre(j, d):
        s = behind(d)
        return remote(mine.at[j, s], theirs.at[j, s], v.s_pre, (j, d), {ROW: 1 - r})

    def sums(j):
        return (v.rs_b, v.rk_b, v.ry_b, v.zs_b, v.zr_b) if j == 0 else (v.rs_f, v.rk_f, v.ry_f, v.zs_f, v.zr_f)

    def rs_k(j, d):
        rs, rk = sums(j)[:2]
        return remote(rs.at[behind(d), 1 - core], rk.at[behind(d)], v.s_rk, (j, d), {COL: 2 * y + 1 - core})

    def rs_y(j, d, g):
        rs, _, ry, _, _ = sums(j)
        s = behind(d)
        return remote(rs.at[s, core, y_up(g)], ry.at[s, y], v.s_ry, (j, d, g), {COL: 2 * y_up(g) + core})

    def rs_y_in(j, d, g):
        here = sums(j)[2].at[behind(d), y_down(g)]
        return remote(here, here, v.s_ry, (j, d, g), {COL: 2 * y_up(g) + core})

    def rs_z(j, d):
        zs, zr = sums(j)[3:]
        return remote(zs.at[d], zr.at[d], v.s_rz, (j, d), {SECTION: ahead(1)})

    def grad_slot(k, s, half):
        return (v.gl_in if k == 0 else v.gr_in).at[half, s]

    def grad_source(k, s, other):
        return (v.gl_out if k == 0 else v.gr_out).at[s, other]

    def halves(other):
        return 1 - r if other else r

    def grad_z(k, d, other=0):
        slot = grad_slot(k, z, halves(other))
        return remote(grad_source(k, behind(d), other), slot, v.s_gz, (2 * other + k, d), {SECTION: behind(d)})

    def grad_z_in(k, d, other=0):
        here = grad_slot(k, ahead(d), halves(other))
        return remote(here, here, v.s_gz, (2 * other + k, d), {SECTION: behind(d)})

    def grad_keep(k, other):
        source = grad_source(k, z, other)
        half = other_half if other else my_half
        target = gl_o.at[at(z, units), half] if k == 0 else gr_o.at[half, at(z, units)]
        return pltpu.make_async_copy(source, target, v.s_put.at[2 * other + k])

    def grad_put(k, d, half):
        s, lanes = ahead(d), pl.ds(half * share, share)
        target = gl_o.at[at(s, units), lanes] if k == 0 else gr_o.at[lanes, at(s, units)]
        return pltpu.make_async_copy(grad_slot(k, s, half), target, v.s_gput.at[k, half, d])

    def grad_x(k, d):
        here = grad_slot(k, ahead(d), r)
        return remote(here, here, v.s_gx, (k, d), {ROW: 1 - r})

    def grad_x_in(k, d):
        here = grad_slot(k, ahead(d), 1 - r)
        return remote(here, here, v.s_gx, (k, d), {ROW: 1 - r})

    def rank_x(j):
        block = pl.ds(0, 2) if j == 0 else pl.ds(2, 1)
        return remote(v.rank_out.at[block], v.rank_in.at[block], v.s_rank_x, (j,), {ROW: 1 - r})

    def rank_c(e):
        here = v.rank_all.at[c]
        return remote(here, here, v.s_rank_c, (e,), {COL: col_up(e)})

    def rank_c_in(e):
        here = v.rank_all.at[col_down(e)]
        return remote(here, here, v.s_rank_c, (e,), {COL: col_up(e)})

    def hand(j):
        if j == 0:
            return remote(v.hand.at[0], hb_o, v.s_hand_z, (0,), {SECTION: behind(1)})
        return remote(v.hand.at[1], hf_o, v.s_hand_z, (1,), {SECTION: ahead(1)})

    def spread(t, d):
        for g in range(1, Y):
            tok_y(t, d, g).start()
        tok_k(t, d, 0).start()

    def forward(t, d):
        tok_z_in(t, d).wait_recv()

        @pl.when(d + 1 < S)
        def _():
            tok_z(t, d + 1).start()

        spread(t, d)

    def forward_all(d):
        for t in (BWD, LOW, COT):
            forward(t, d)

        @pl.when(d + 1 < S)
        def _():
            for k in range(2):
                fac(k, d + 1).start()

        forward(FWD, d)

    def send(d, low_too=True):
        for t in (BWD, COT, LOW) if low_too else (BWD, COT):
            tok_z(t, d).start()
        for k in range(2):
            fac(k, d).start()
        tok_z(FWD, d).start()

    def gathered(t, d):
        for g in range(1, Y):
            tok_y_in(t, d, g).wait_recv()
            tok_k(t, d, g).start()
        for g in range(Y):
            tok_k_in(t, d, g).wait_recv()

    def tokens(t, s):
        return tok[t, s].reshape(micro, width)

    def rank_tokens(t, s, half=r):
        return low[s, :, 4 if t == FWD else 2 * t + half].reshape(micro, share)

    def partial_up(j, t, d):
        s = behind(d)

        @pl.loop(0, units // min(TILE, units))
        def _(n):
            cols = at(n, min(TILE, units))
            part = nn(tokens(t, s), wu[:, cols]) + nn(rank_tokens(t, s), rt[s, :, cols])
            mine[j, s, :, cols] = part.astype(BF16)

        pre(j, d).start()

    def partial_down(d):
        s = behind(d)

        @pl.loop(0, units // min(TILE, units))
        def _(n):
            cols = at(n, min(TILE, units))
            part = nt(tokens(COT, s), wd[cols, :]) + nt(rank_tokens(COT, s), lt[s, cols, :])
            mine[1, s, :, cols] = part.astype(BF16)

        pre(1, d).start()

    def bwd_partials(d, first):
        gathered(BWD, d)
        gathered(LOW, d)
        if not first:
            fac_in(0, d).wait_recv()
        partial_up(0, BWD, d)
        gathered(COT, d)
        if not first:
            fac_in(1, d).wait_recv()
        partial_down(d)

    def fwd_partials(d):
        gathered(FWD, d)
        partial_up(2, FWD, d)

    def by_owner(rs, s, cols, part):
        part = part.astype(BF16)
        for col in range(C):
            rs[s, col % 2, col // 2, :, cols] = part[col * own : (col + 1) * own]

    def bwd_chunk(d):
        s = behind(d)
        for j in range(2):
            pre(j, d).wait()

        @pl.loop(0, units // min(TILE, units))
        def _(n):
            cols = at(n, min(TILE, units))
            p = mine[0, s, :, cols].astype(F32) + theirs[0, s, :, cols].astype(F32)
            g = mine[1, s, :, cols].astype(F32) + theirs[1, s, :, cols].astype(F32)
            sigma = jax.nn.sigmoid(p)
            mine[0, s, :, cols] = (p * sigma).astype(BF16)
            mine[1, s, :, cols] = (g * (sigma * (1.0 + p * (1.0 - sigma)))).astype(BF16)

        @pl.loop(0, width // TILE)
        def _(n):
            cols = at(n, TILE)
            by_owner(v.rs_b, s, cols, nt(mine[1, s], wu[cols, :]))

        by_owner(v.rs_b, s, slice(width, width + share), nt(mine[1, s], rt[s]))
        by_owner(v.rs_b, s, slice(width + share, width + 2 * share), nn(mine[0, s], lt[s]))
        rs_k(0, d).start()
        v.gl_out[s, 0] = tn(mine[0, s], rank_tokens(COT, s)).astype(BF16)
        v.gr_out[s, 0] = tn(rank_tokens(BWD, s), mine[1, s]).astype(BF16)

        @pl.when((d > 0) & (d + 2 >= S))
        def _():
            for k in range(2):
                grad_z(k, d).start()

        @pl.when(d < FULL)
        def _():
            v.gl_out[s, 1] = tn(mine[0, s], rank_tokens(COT, s, 1 - r)).astype(BF16)
            v.gr_out[s, 1] = tn(rank_tokens(BWD, s, 1 - r), mine[1, s]).astype(BF16)

        @pl.when((d < FULL) & (d > 0))
        def _():
            for k in range(2):
                grad_z(k, d, 1).start()

        @pl.when(d == 0)
        def _():
            for k in range(2):
                for other in range(2):
                    grad_keep(k, other).start()

    def fwd_chunk(d):
        s = behind(d)
        pre(2, d).wait()

        @pl.loop(0, units // min(TILE, units))
        def _(n):
            cols = at(n, min(TILE, units))
            p = mine[2, s, :, cols].astype(F32) + theirs[2, s, :, cols].astype(F32)
            mine[2, s, :, cols] = (p * jax.nn.sigmoid(p)).astype(BF16)

        @pl.loop(0, width // TILE)
        def _(n):
            cols = at(n, TILE)
            by_owner(v.rs_f, s, cols, nn(mine[2, s], wd[:, cols]))

        by_owner(v.rs_f, s, slice(width, width + share), nn(mine[2, s], lt[s]))
        rs_k(1, d).start()

    def reduce_core(j, d):
        s = behind(d)
        rs, rk = sums(j)[:2]
        rs_k(j, d).wait()
        rs[s, core] = (rs[s, core].astype(F32) + rk[s].astype(F32)).astype(BF16)
        for g in range(1, Y):
            rs_y(j, d, g).start()

    def reduce_chunk(j, d):
        s = behind(d)
        rs, _, ry, zs, zr = sums(j)
        total = rs[s, core, y].astype(F32)
        for g in range(1, Y):
            rs_y_in(j, d, g).wait_recv()
            total = total + ry[s, y_down(g)].astype(F32)

        @pl.when(d == 0)
        def _():
            zr[0] = total.astype(BF16)

        @pl.when(d == 1)
        def _():
            zs[1] = total.astype(BF16)
            rs_z(j, 1).start()

        @pl.when(d > 1)
        def _():
            rs_z(j, d - 1).wait_recv()
            zs[d] = (total + zr[d - 1].astype(F32)).astype(BF16)
            rs_z(j, d).start()

    def pass_on(d):
        for k in range(2):
            grad_z_in(k, d).wait_recv()
            grad_x(k, d).start()

    def home_sum(j):
        zr = sums(j)[4]
        rs_z(j, S - 1).wait_recv()
        return zr[0].astype(F32) + zr[S - 1].astype(F32)

    def grad_up():
        step = min(TILE, units)

        @pl.loop(0, width // TILE)
        def _(m):
            slot = lax.rem(m, 2)
            put = pltpu.make_async_copy(v.gu_tile.at[slot], gu_o.at[at(m, TILE), :], v.s_gu_put.at[slot])

            @pl.when(m >= 2)
            def _():
                put.wait()

            for n in range(units // step):
                left = tok[BWD, :, :, :, at(m, TILE)].reshape(S * micro, TILE)
                right = mine[1, :, :, n * step : (n + 1) * step].reshape(S * micro, step)
                v.gu_tile[slot, :, n * step : (n + 1) * step] = tn(left, right).astype(BF16)
            put.start()

    def grad_down():
        tall = min(TILE, units)

        @pl.loop(0, units // tall)
        def _(m):
            slot = lax.rem(m, 2)
            put = pltpu.make_async_copy(
                v.gd_tile.at[slot, :tall], gd_o.at[at(m, tall), :], v.s_gd_put.at[slot]
            )

            @pl.when(m >= 2)
            def _():
                put.wait()

            for n in range(width // TILE):
                left = mine[0, :, :, at(m, tall)].reshape(S * micro, tall)
                right = tok[COT, :, :, :, n * TILE : (n + 1) * TILE].reshape(S * micro, TILE)
                v.gd_tile[slot, :tall, n * TILE : (n + 1) * TILE] = tn(left, right).astype(BF16)
            put.start()

    def drain_tiles(sem, tile, out, tall, count):
        for m in range(max(0, count - 2), count):
            pltpu.make_async_copy(
                tile.at[m % 2, :tall], out.at[m * tall : (m + 1) * tall, :], sem.at[m % 2]
            ).wait()

    loads = [
        (xb_h, tok.at[BWD, z, c]),
        (ct_h, tok.at[COT, z, c]),
        (xf_h, tok.at[FWD, z, c]),
        (ul_h, ul),
        (dr_h, dr),
        (wu_h, wu),
        (ur_h.at[my_half, at(z, units)], rt.at[z]),
        (wd_h, wd),
        (dl_h.at[at(z, units), my_half], lt.at[z]),
    ]
    loads = [pltpu.make_async_copy(a, b, v.s_load.at[i]) for i, (a, b) in enumerate(loads)]
    for copy in loads:
        copy.start()
    barrier = pltpu.get_barrier_semaphore()
    pl.semaphore_signal(barrier, inc=1, device_id={ROW: 1 - r}, device_id_type=MESH)
    for e in range(1, C):
        pl.semaphore_signal(barrier, inc=1, device_id={COL: col_up(e)}, device_id_type=MESH)
    for d in range(1, S):
        pl.semaphore_signal(barrier, inc=1, device_id={SECTION: ahead(d)}, device_id_type=MESH)
    for copy in loads[:3]:
        copy.wait()
    pl.semaphore_wait(barrier, S + C - 1)

    spread(BWD, 0)
    spread(COT, 0)
    send(1, False)
    for copy in loads[3:5]:
        copy.wait()
    v.low_part[BWD] = nn(tok[BWD, z, c], ul[...]).astype(BF16)
    v.low_part[COT] = nt(tok[COT, z, c], dr[...]).astype(BF16)
    v.low_part[FWD] = nn(tok[FWD, z, c], ul[...]).astype(BF16)
    low_x().start()
    low_x().wait()
    for t in (BWD, COT):
        for half in range(2):
            cols = pl.ds(half * share, share)
            low[z, c, 2 * t + half] = (v.low_part[t, :, cols].astype(F32) + v.low_in[t, :, cols].astype(F32)).astype(BF16)
    low[z, c, 4] = (v.low_part[FWD, :, my_half].astype(F32) + v.low_in[FWD, :, my_half].astype(F32)).astype(BF16)
    spread(LOW, 0)
    tok_z(LOW, 1).start()
    spread(FWD, 0)
    for copy in loads[5:]:
        copy.wait()
    bwd_partials(0, True)
    fwd_partials(0)
    forward_all(1)

    @pl.loop(0, S)
    def _(i):
        @pl.when(i + 1 < S)
        def _():
            bwd_partials(i + 1, False)

        @pl.when(i + 1 == S)
        def _():
            @pl.loop(1, S)
            def _(d):
                fwd_partials(d)

        @pl.when(i > 0)
        def _():
            reduce_chunk(0, i - 1)

        bwd_chunk(i)
        reduce_core(0, i)

        @pl.when(i == 0)
        def _():
            fwd_chunk(0)
            reduce_core(1, 0)

        @pl.when(i + 2 < S)
        def _():
            forward_all(i + 2)

        @pl.when((i > 0) & (i + 2 < S))
        def _():
            for k in range(2):
                grad_z(k, i).start()

    reduce_chunk(0, S - 1)
    grad_up()

    @pl.loop(1, S)
    def _(i):
        fwd_chunk(i)
        reduce_core(1, i)
        reduce_chunk(1, i - 1)

        @pl.when((i >= FULL) & (i + 1 < S))
        def _():
            pass_on(i)

    reduce_chunk(1, S - 1)

    total = home_sum(0)
    v.rank_out[0] = total[:, width : width + share].astype(BF16)
    v.rank_out[1] = total[:, width + share :].astype(BF16)
    rank_x(0).start()
    grad_norm = total[:, :width] + tok[COT, z, c].astype(F32)
    total = home_sum(1)
    v.rank_out[2] = total[:, width:].astype(BF16)
    rank_x(1).start()
    out = total[:, :width] + tok[FWD, z, c].astype(F32)
    rank_x(0).wait()
    v.rank_all[c, :, :, my_half] = v.rank_out[0:2]
    v.rank_all[c, :, :, other_half] = v.rank_in[0:2]
    for e in range(1, C):
        rank_c(e).start()
    v.hand[0] = (grad_norm + nt(v.rank_all[c, 0], ul[...])).astype(BF16)
    hand(0).start()
    rank_x(1).wait()
    out = out + nn(v.rank_out[2], dr[my_half, :]) + nn(v.rank_in[2], dr[other_half, :])
    v.hand[1] = out.astype(BF16)
    hand(1).start()
    for d in range(S - 1, S):
        pass_on(d)
    for e in range(1, C):
        rank_c_in(e).wait_recv()
    v.gul[...] = tn(tokens(BWD, z), v.rank_all[:, 0].reshape(micro, rank))
    put_up = pltpu.make_async_copy(v.gul, gul_o, v.s_put.at[4])
    put_up.start()
    v.gdr[...] = tn(v.rank_all[:, 1].reshape(micro, rank), tokens(COT, z))
    put_down = pltpu.make_async_copy(v.gdr, gdr_o, v.s_put.at[5])
    put_down.start()
    grad_down()

    for k in range(2):
        for other in range(2):
            grad_keep(k, other).wait()
        for d in range(1, FULL):
            grad_z_in(k, d).wait_recv()
            grad_z_in(k, d, 1).wait_recv()
            grad_z(k, d, 1).wait_send()
            for half in range(2):
                grad_put(k, d, half).start()

    @pl.loop(FULL, S)
    def _(d):
        for k in range(2):
            grad_x(k, d).wait_send()
            grad_x_in(k, d).wait_recv()
            for half in range(2):
                grad_put(k, d, half).start()

    tall = min(TILE, units)
    drain_tiles(v.s_gu_put, v.gu_tile, gu_o, TILE, width // TILE)
    drain_tiles(v.s_gd_put, v.gd_tile, gd_o, tall, units // tall)
    put_up.wait()
    put_down.wait()

    @pl.loop(1, S)
    def _(d):
        for t in range(4):
            tok_z(t, d).wait_send()
        for k in range(2):
            fac(k, d).wait_send()
            grad_z(k, d).wait_send()
            rs_z(k, d).wait_send()

    @pl.loop(0, S)
    def _(d):
        for t in range(4):
            for g in range(Y):
                tok_k(t, d, g).wait_send()
            for g in range(1, Y):
                tok_y(t, d, g).wait_send()
        for j in range(2):
            for g in range(1, Y):
                rs_y(j, d, g).wait_send()

    for e in range(1, C):
        rank_c(e).wait_send()
    for j in range(2):
        hand(j).wait()

    @pl.loop(1, S)
    def _(d):
        for k in range(2):
            for half in range(2):
                grad_put(k, d, half).wait()


def finish_kernel(count, *refs):
    ins, outs, near, wide = refs[:8], refs[8:16], refs[16:24], refs[24:26]
    s_in, s_out = refs[26:]
    pieces = []
    for i in (5, 6, 2, 3, 4, 7, 0, 1):
        parts = count if i in (2, 3, 5, 6) else 1
        tall = ins[i].shape[0] // parts
        for p in range(parts):
            rows = pl.ds(p * tall, tall)
            final = wide[i - 5] if i in (5, 6) else near[i]
            load = pltpu.make_async_copy(ins[i].at[rows], near[i].at[rows], s_in.at[i, p])
            store = pltpu.make_async_copy(final.at[rows], outs[i].at[rows], s_out.at[i, p])
            pieces.append((i, rows, load, store))
    for _, _, load, _ in pieces:
        load.start()
    for i, rows, load, store in pieces:
        load.wait()
        if i in (5, 6):
            wide[i - 5][rows] = near[i][rows].astype(F32)
        store.start()
    for _, _, _, store in pieces:
        store.wait()


def finish(arrays):
    whole, count = pl.BlockSpec(memory_space=pl.ANY), 4
    outs = [jax.ShapeDtypeStruct(a.shape, F32 if i in (5, 6) else a.dtype) for i, a in enumerate(arrays)]
    return pl.pallas_call(
        functools.partial(finish_kernel, count),
        out_shape=outs,
        in_specs=[whole] * len(outs),
        out_specs=[whole] * len(outs),
        scratch_shapes=[pltpu.VMEM(a.shape, a.dtype) for a in arrays]
        + [pltpu.VMEM(outs[i].shape, F32) for i in (5, 6)]
        + [pltpu.SemaphoreType.DMA((8, count))] * 2,
        compiler_params=pltpu.CompilerParams(vmem_limit_bytes=VMEM_BYTES),
    )(*arrays)


def fused(*args):
    S, C = lax.axis_size(SECTION), lax.axis_size(COL)
    own, width = args[0].shape[1:]
    units, rank = args[3].shape[1], args[5].shape[2]
    shapes = scratch_of(S, C, own, width, units, rank)
    outs = [
        ((own, width), BF16),
        ((own, width), BF16),
        ((width, units), BF16),
        ((units, width), BF16),
        ((width, rank), F32),
        ((S * units, rank), BF16),
        ((rank, S * units), BF16),
        ((rank, width), F32),
    ]
    whole = pl.BlockSpec(memory_space=pl.ANY)
    tokens = 3 * S * own * C
    outputs = pl.pallas_call(
        functools.partial(kernel, S, C, list(shapes)),
        out_shape=[jax.ShapeDtypeStruct(*out) for out in outs],
        in_specs=[whole] * len(args),
        out_specs=[whole] * len(outs),
        scratch_shapes=list(shapes.values()),
        compiler_params=pltpu.CompilerParams(
            collective_id=0, has_side_effects=True, vmem_limit_bytes=VMEM_BYTES
        ),
        cost_estimate=pl.CostEstimate(
            flops=6 * tokens * width * units, bytes_accessed=20 * width * units, transcendentals=tokens * units
        ),
    )(*[arg[0] if arg.ndim == 3 else arg for arg in args])
    hand_f, hand_b, grad_up, grad_down, grad_ul, grad_dl, grad_ur, grad_dr = finish(outputs)
    return (
        hand_f[None],
        hand_b[None],
        grad_up,
        grad_down,
        grad_ul[None],
        grad_ur[None],
        grad_dl[None],
        grad_dr[None],
    )


def step(*args):
    S, C, rows = (lax.axis_size(axis) for axis in (SECTION, COL, ROW))
    own, width = args[0].shape[1:]
    units, rank = args[3].shape[1], args[5].shape[2]
    shapes = scratch_of(S, C, own, width, units, rank)
    fits = vmem_need(shapes) <= VMEM_BYTES - (2 << 20)
    even = rows == 2 and S > 2 and C % 2 == 0 and width % TILE == 0 and (units % TILE == 0 or units == 128)
    if fits and even and rank == 256 and own % 16 == 0:
        return fused(*args)
    return local(*args)


def solution(mesh):
    in_specs = (
        P("section", "col", "row"),
        P("section", "col", "row"),
        P("section", "col", "row"),
        P("row", ("col", "section")),
        P(("col", "section"), "row"),
        P("section", "row", None),
        P("section", None, "col"),
        P("section", "col", None),
        P("section", None, "row"),
    )
    out_specs = (
        P("section", "col", "row"),
        P("section", "col", "row"),
        P("row", ("col", "section")),
        P(("col", "section"), "row"),
        P("section", "row", None),
        P("section", None, "col"),
        P("section", "col", None),
        P("section", None, "row"),
    )
    return jax.shard_map(step, mesh=mesh, in_specs=in_specs, out_specs=out_specs, check_vma=False)
```

```python
import functools
import types

import jax
import jax.numpy as jnp
from jax import lax
from jax.experimental import pallas as pl
from jax.experimental.pallas import tpu as pltpu
from jax.sharding import PartitionSpec as P

F32, BF16 = jnp.float32, jnp.bfloat16


def from_behind(block, axis, distance):
    count = lax.axis_size(axis)
    return lax.ppermute(block, axis, [((i - distance) % count, i) for i in range(count)])


def row_sum(part):
    total = part.astype(F32)
    for step in range(1, lax.axis_size("row")):
        total = total + from_behind(part, "row", step).astype(F32)
    return total


def row_gather(block, axis):
    count, me = lax.axis_size("row"), lax.axis_index("row")
    wide = jnp.zeros(block.shape[:axis] + (count * block.shape[axis],) + block.shape[axis + 1 :], block.dtype)
    for step in range(count):
        piece = block if step == 0 else from_behind(block, "row", step)
        origin = (me - step) % count
        wide = lax.dynamic_update_slice_in_dim(wide, piece, origin * block.shape[axis], axis)
    return wide


def mm(spec, left, right):
    return jnp.einsum(spec, left, right, preferred_element_type=F32)


def silu_slope(preact):
    sigma = jax.nn.sigmoid(preact)
    return sigma * (1.0 + preact * (1.0 - sigma))


def local(
    input_fwd,
    input_bwd,
    cotangent,
    shared_up,
    shared_down,
    up_left,
    up_right,
    down_left,
    down_right,
):
    sections, rows = lax.axis_size("section"), lax.axis_size("row")
    section, row = lax.axis_index("section"), lax.axis_index("row")
    own, width = input_fwd.shape[1], input_fwd.shape[2]
    units = shared_up.shape[1]
    share = up_left.shape[2] // rows
    everyone = ("section", "col")
    micro = own * lax.axis_size("col")

    def own_share(block, axis):
        return lax.dynamic_slice_in_dim(block, row * share, share, axis)

    def own_section(tokens):
        return lax.dynamic_slice_in_dim(tokens, section * micro, micro, 0)

    def per_section(tokens):
        return tokens.reshape(sections, micro, tokens.shape[-1])

    x_fwd, x_bwd, cot = input_fwd[0], input_bwd[0], cotangent[0]
    all_bwd = lax.all_gather(x_bwd, everyone, axis=0, tiled=True)
    all_cot = lax.all_gather(cot, everyone, axis=0, tiled=True)
    all_fwd = lax.all_gather(x_fwd, everyone, axis=0, tiled=True)

    din_part = mm("tmd,dr->tmr", jnp.stack([x_fwd, x_bwd]), up_left[0])
    gdout_part = mm("md,rd->mr", cot, down_right[0])
    low_part = jnp.concatenate([din_part, gdout_part[None]]).astype(BF16)
    low = own_share(row_sum(low_part).astype(BF16), 2)
    low_all = lax.all_gather(low, everyone, axis=1, tiled=True)
    din_fwd, din_bwd, gdout = (per_section(low_all[i]) for i in range(3))

    right = lax.all_to_all(own_share(up_right[0], 0), "section", 1, 0, tiled=True)
    right = right.reshape(sections, share, units)
    left = lax.all_to_all(own_share(down_left[0], 0 + 1), "section", 0, 0, tiled=True)
    left = left.reshape(sections, units, share)

    def preact_of(tokens, din):
        part = mm("smd,df->smf", per_section(tokens), shared_up) + mm("smr,srf->smf", din, right)
        return row_sum(part.astype(BF16))

    pre_bwd = preact_of(all_bwd, din_bwd)
    ghid_part = mm("smd,fd->smf", per_section(all_cot), shared_down) + mm("smr,sfr->smf", gdout, left)
    grad_hidden = row_sum(ghid_part.astype(BF16))
    hid_bwd = jax.nn.silu(pre_bwd).astype(BF16)
    gpre = (grad_hidden * silu_slope(pre_bwd)).astype(BF16)
    flat_gpre = gpre.reshape(sections * micro, units)

    gnorm_part = mm("mf,df->md", flat_gpre, shared_up)
    gdin_part = mm("smf,srf->smr", gpre, right).reshape(sections * micro, share)
    back_part = jnp.concatenate([gnorm_part.astype(BF16), gdin_part.astype(BF16)], axis=1)
    back = lax.psum_scatter(back_part, everyone, scatter_dimension=0, tiled=True)
    gdin_own = row_gather(back[:, width:], 1)

    pre_fwd = preact_of(all_fwd, din_fwd)
    hid_fwd = jax.nn.silu(pre_fwd).astype(BF16)
    out_part = mm("mf,fd->md", hid_fwd.reshape(sections * micro, units), shared_down)
    dout_part = [
        mm("smf,sfr->smr", h, left).reshape(sections * micro, share).astype(BF16) for h in (hid_fwd, hid_bwd)
    ]
    ahead_part = jnp.concatenate([out_part.astype(BF16), *dout_part], axis=1)
    ahead = lax.psum_scatter(ahead_part, everyone, scatter_dimension=0, tiled=True)
    dout_own = row_gather(ahead[:, width:].reshape(own, 2, share), 2)

    grad_up = mm("md,mf->df", all_bwd, flat_gpre).astype(BF16)
    grad_down = mm("mf,md->fd", hid_bwd.reshape(sections * micro, units), all_cot).astype(BF16)

    grad_left = mm("smf,smr->sfr", hid_bwd, gdout).astype(BF16).reshape(sections * units, share)
    grad_left = lax.all_to_all(grad_left, "section", 0, 0, tiled=True)
    grad_down_left = row_gather(grad_left, 1).astype(F32)
    grad_right = mm("smr,smf->srf", din_bwd, gpre).astype(BF16).reshape(sections * share, units)
    grad_right = lax.all_to_all(grad_right, "section", 0, 1, tiled=True)
    grad_up_right = row_gather(grad_right, 0).astype(F32)

    grad_input = (
        cot.astype(F32) + back[:, :width].astype(F32) + mm("mr,dr->md", gdin_own, up_left[0])
    )
    handoff_bwd = from_behind(grad_input.astype(BF16)[None], "section", -1)
    gdin_all = lax.all_gather(gdin_own, "col", axis=0, tiled=True)
    grad_up_left = mm("md,mr->dr", own_section(all_bwd), gdin_all)

    out_fwd = (
        x_fwd.astype(F32) + ahead[:, :width].astype(F32) + mm("mr,rd->md", dout_own[:, 0], down_right[0])
    )
    handoff_fwd = from_behind(out_fwd.astype(BF16)[None], "section", 1)
    dout_all = lax.all_gather(dout_own[:, 1], "col", axis=0, tiled=True)
    grad_down_right = mm("mr,md->rd", dout_all, own_section(all_cot))
    return (
        handoff_fwd,
        handoff_bwd,
        grad_up,
        grad_down,
        grad_up_left[None],
        grad_up_right[None],
        grad_down_left[None],
        grad_down_right[None],
    )


MESH = pl.DeviceIdType.MESH
SECTION, ROW, COL = "section", "row", "col"
BWD, COT, FWD, LOW = range(4)
TILE = 256
FULL = 1
VMEM_BYTES = 63 * 1024 * 1024


def nn(left, right):
    return lax.dot_general(left, right, (((1,), (0,)), ((), ())), preferred_element_type=F32)


def nt(left, right):
    return lax.dot_general(left, right, (((1,), (1,)), ((), ())), preferred_element_type=F32)


def tn(left, right):
    return lax.dot_general(left, right, (((0,), (0,)), ((), ())), preferred_element_type=F32)


def at(index, size):
    return pl.ds(pl.multiple_of(index * size, size), size)


def scratch_of(S, C, own, width, units, rank):
    share, micro = rank // 2, own * C
    wide_b, wide_f = width + 2 * share, width + share
    arrays = dict(
        tok=(3, S, C, own, width),
        low=(S, C, 5, own, share),
        low_part=(3, own, rank),
        low_in=(3, own, rank),
        rt=(S, share, units),
        lt=(S, units, share),
        wu=(width, units),
        wd=(units, width),
        ul=(width, rank),
        dr=(rank, width),
        mine=(3, S, micro, units),
        theirs=(3, S, micro, units),
        rs_b=(S, 2, C // 2, own, wide_b),
        rk_b=(S, C // 2, own, wide_b),
        ry_b=(S, C // 2, own, wide_b),
        rs_f=(S, 2, C // 2, own, wide_f),
        rk_f=(S, C // 2, own, wide_f),
        ry_f=(S, C // 2, own, wide_f),
        zs_b=(S, own, wide_b),
        zr_b=(S, own, wide_b),
        zs_f=(S, own, wide_f),
        zr_f=(S, own, wide_f),
        gl_out=(S, 2, units, share),
        gr_out=(S, 2, share, units),
        gl_in=(2, S, units, share),
        gr_in=(2, S, share, units),
        gu_tile=(2, TILE, units),
        gd_tile=(2, TILE, width),
        rank_out=(3, own, share),
        rank_in=(3, own, share),
        rank_all=(C, 2, own, rank),
        hand=(2, own, width),
    )
    shapes = {name: pltpu.VMEM(shape, BF16) for name, shape in arrays.items()}
    shapes["gul"] = pltpu.VMEM((width, rank), F32)
    shapes["gdr"] = pltpu.VMEM((rank, width), F32)
    sems = dict(
        s_load=(12,),
        s_put=(6,),
        s_gput=(2, 2, S),
        s_gu_put=(2,),
        s_gd_put=(2,),
        s_tz=(2, 4, S),
        s_ty=(2, 4, S, C // 2),
        s_tk=(2, 4, S, C // 2),
        s_fac=(2, 2, S),
        s_low_x=(2,),
        s_pre=(2, 3, S),
        s_rk=(2, 2, S),
        s_ry=(2, 2, S, C // 2),
        s_rz=(2, 2, S),
        s_gz=(2, 4, S),
        s_gx=(2, 2, S),
        s_rank_x=(2, 2),
        s_rank_c=(2, C),
        s_hand_z=(2, 2),
    )
    for name, shape in sems.items():
        shapes[name] = pltpu.SemaphoreType.DMA(shape)
    return shapes


def vmem_need(shapes):
    total = 0
    for name, ref in shapes.items():
        if not name.startswith("s_"):
            size = jnp.dtype(ref.dtype).itemsize
            for extent in ref.shape:
                size *= extent
            total += size
    return total


def kernel(S, C, names, *refs):
    xf_h, xb_h, ct_h, wu_h, wd_h, ul_h, ur_h, dl_h, dr_h = refs[:9]
    hf_o, hb_o, gu_o, gd_o, gul_o, gl_o, gr_o, gdr_o = refs[9:17]
    v = types.SimpleNamespace(**dict(zip(names, refs[17:])))
    tok, low, rt, lt, mine, theirs = v.tok, v.low, v.rt, v.lt, v.mine, v.theirs
    wu, wd, ul, dr = v.wu, v.wd, v.ul, v.dr
    own, width = tok.shape[3], tok.shape[4]
    units, share = lt.shape[1], lt.shape[2]
    rank, micro, Y = 2 * share, own * C, C // 2
    z, r, c = (lax.axis_index(axis) for axis in (SECTION, ROW, COL))
    y, core = c // 2, lax.rem(c, 2)
    my_half, other_half = at(r, share), at(1 - r, share)

    def behind(d):
        return lax.rem(z - d + S, S)

    def ahead(d):
        return lax.rem(z + d, S)

    def col_up(e):
        return lax.rem(c + e, C)

    def col_down(e):
        return lax.rem(c - e + C, C)

    def y_up(g):
        return lax.rem(y + g, Y)

    def y_down(g):
        return lax.rem(y - g + Y, Y)

    def remote(source, target, sem, index, where):
        return pltpu.make_async_remote_copy(
            src_ref=source,
            dst_ref=target,
            send_sem=sem.at[(0,) + index],
            recv_sem=sem.at[(1,) + index],
            device_id=where,
            device_id_type=MESH,
        )

    def piece(t, s, col):
        return low.at[s, col] if t == LOW else tok.at[t, s, col]

    def tok_z(t, d):
        here = piece(t, behind(d - 1), c)
        return remote(here, here, v.s_tz, (t, d), {SECTION: ahead(1)})

    def tok_z_in(t, d):
        here = piece(t, behind(d), c)
        return remote(here, here, v.s_tz, (t, d), {SECTION: ahead(1)})

    def tok_y(t, d, g):
        here = piece(t, behind(d), c)
        return remote(here, here, v.s_ty, (t, d, g), {COL: 2 * y_up(g) + core})

    def tok_y_in(t, d, g):
        here = piece(t, behind(d), 2 * y_down(g) + core)
        return remote(here, here, v.s_ty, (t, d, g), {COL: 2 * y_up(g) + core})

    def tok_k(t, d, g):
        here = piece(t, behind(d), 2 * y_down(g) + core)
        return remote(here, here, v.s_tk, (t, d, g), {COL: 2 * y + 1 - core})

    def tok_k_in(t, d, g):
        here = piece(t, behind(d), 2 * y_down(g) + 1 - core)
        return remote(here, here, v.s_tk, (t, d, g), {COL: 2 * y + 1 - core})

    def fac(k, d):
        if k == 0:
            return remote(ur_h.at[my_half, at(ahead(d), units)], rt.at[z], v.s_fac, (0, d), {SECTION: ahead(d)})
        return remote(dl_h.at[at(ahead(d), units), my_half], lt.at[z], v.s_fac, (1, d), {SECTION: ahead(d)})

    def fac_in(k, d):
        here = (rt if k == 0 else lt).at[behind(d)]
        return remote(here, here, v.s_fac, (k, d), {SECTION: ahead(d)})

    def low_x():
        return remote(v.low_part, v.low_in, v.s_low_x, (), {ROW: 1 - r})

    def pre(j, d):
        s = behind(d)
        return remote(mine.at[j, s], theirs.at[j, s], v.s_pre, (j, d), {ROW: 1 - r})

    def sums(j):
        return (v.rs_b, v.rk_b, v.ry_b, v.zs_b, v.zr_b) if j == 0 else (v.rs_f, v.rk_f, v.ry_f, v.zs_f, v.zr_f)

    def rs_k(j, d):
        rs, rk = sums(j)[:2]
        return remote(rs.at[behind(d), 1 - core], rk.at[behind(d)], v.s_rk, (j, d), {COL: 2 * y + 1 - core})

    def rs_y(j, d, g):
        rs, _, ry, _, _ = sums(j)
        s = behind(d)
        return remote(rs.at[s, core, y_up(g)], ry.at[s, y], v.s_ry, (j, d, g), {COL: 2 * y_up(g) + core})

    def rs_y_in(j, d, g):
        here = sums(j)[2].at[behind(d), y_down(g)]
        return remote(here, here, v.s_ry, (j, d, g), {COL: 2 * y_up(g) + core})

    def rs_z(j, d):
        zs, zr = sums(j)[3:]
        return remote(zs.at[d], zr.at[d], v.s_rz, (j, d), {SECTION: ahead(1)})

    def grad_slot(k, s, half):
        return (v.gl_in if k == 0 else v.gr_in).at[half, s]

    def grad_source(k, s, other):
        return (v.gl_out if k == 0 else v.gr_out).at[s, other]

    def halves(other):
        return 1 - r if other else r

    def grad_z(k, d, other=0):
        slot = grad_slot(k, z, halves(other))
        return remote(grad_source(k, behind(d), other), slot, v.s_gz, (2 * other + k, d), {SECTION: behind(d)})

    def grad_z_in(k, d, other=0):
        here = grad_slot(k, ahead(d), halves(other))
        return remote(here, here, v.s_gz, (2 * other + k, d), {SECTION: behind(d)})

    def grad_keep(k, other):
        source = grad_source(k, z, other)
        half = other_half if other else my_half
        target = gl_o.at[at(z, units), half] if k == 0 else gr_o.at[half, at(z, units)]
        return pltpu.make_async_copy(source, target, v.s_put.at[2 * other + k])

    def grad_put(k, d, half):
        s, lanes = ahead(d), pl.ds(half * share, share)
        target = gl_o.at[at(s, units), lanes] if k == 0 else gr_o.at[lanes, at(s, units)]
        return pltpu.make_async_copy(grad_slot(k, s, half), target, v.s_gput.at[k, half, d])

    def grad_x(k, d):
        here = grad_slot(k, ahead(d), r)
        return remote(here, here, v.s_gx, (k, d), {ROW: 1 - r})

    def grad_x_in(k, d):
        here = grad_slot(k, ahead(d), 1 - r)
        return remote(here, here, v.s_gx, (k, d), {ROW: 1 - r})

    def rank_x(j):
        block = pl.ds(0, 2) if j == 0 else pl.ds(2, 1)
        return remote(v.rank_out.at[block], v.rank_in.at[block], v.s_rank_x, (j,), {ROW: 1 - r})

    def rank_c(e):
        here = v.rank_all.at[c]
        return remote(here, here, v.s_rank_c, (e,), {COL: col_up(e)})

    def rank_c_in(e):
        here = v.rank_all.at[col_down(e)]
        return remote(here, here, v.s_rank_c, (e,), {COL: col_up(e)})

    def hand(j):
        if j == 0:
            return remote(v.hand.at[0], hb_o, v.s_hand_z, (0,), {SECTION: behind(1)})
        return remote(v.hand.at[1], hf_o, v.s_hand_z, (1,), {SECTION: ahead(1)})

    def spread(t, d):
        for g in range(1, Y):
            tok_y(t, d, g).start()
        tok_k(t, d, 0).start()

    def forward(t, d):
        tok_z_in(t, d).wait_recv()

        @pl.when(d + 1 < S)
        def _():
            tok_z(t, d + 1).start()

        spread(t, d)

    def forward_all(d):
        for t in (BWD, LOW, COT):
            forward(t, d)

        @pl.when(d + 1 < S)
        def _():
            for k in range(2):
                fac(k, d + 1).start()

        forward(FWD, d)

    def send(d, low_too=True):
        for t in (BWD, COT, LOW) if low_too else (BWD, COT):
            tok_z(t, d).start()
        for k in range(2):
            fac(k, d).start()
        tok_z(FWD, d).start()

    def gathered(t, d):
        for g in range(1, Y):
            tok_y_in(t, d, g).wait_recv()
            tok_k(t, d, g).start()
        for g in range(Y):
            tok_k_in(t, d, g).wait_recv()

    def tokens(t, s):
        return tok[t, s].reshape(micro, width)

    def rank_tokens(t, s, half=r):
        return low[s, :, 4 if t == FWD else 2 * t + half].reshape(micro, share)

    def partial_up(j, t, d):
        s = behind(d)

        @pl.loop(0, units // min(TILE, units))
        def _(n):
            cols = at(n, min(TILE, units))
            part = nn(tokens(t, s), wu[:, cols]) + nn(rank_tokens(t, s), rt[s, :, cols])
            mine[j, s, :, cols] = part.astype(BF16)

        pre(j, d).start()

    def partial_down(d):
        s = behind(d)

        @pl.loop(0, units // min(TILE, units))
        def _(n):
            cols = at(n, min(TILE, units))
            part = nt(tokens(COT, s), wd[cols, :]) + nt(rank_tokens(COT, s), lt[s, cols, :])
            mine[1, s, :, cols] = part.astype(BF16)

        pre(1, d).start()

    def bwd_partials(d, first):
        gathered(BWD, d)
        gathered(LOW, d)
        if not first:
            fac_in(0, d).wait_recv()
        partial_up(0, BWD, d)
        gathered(COT, d)
        if not first:
            fac_in(1, d).wait_recv()
        partial_down(d)

    def fwd_partials(d):
        gathered(FWD, d)
        partial_up(2, FWD, d)

    def by_owner(rs, s, cols, part):
        part = part.astype(BF16)
        for col in range(C):
            rs[s, col % 2, col // 2, :, cols] = part[col * own : (col + 1) * own]

    def bwd_chunk(d):
        s = behind(d)
        for j in range(2):
            pre(j, d).wait()

        @pl.loop(0, units // min(TILE, units))
        def _(n):
            cols = at(n, min(TILE, units))
            p = mine[0, s, :, cols].astype(F32) + theirs[0, s, :, cols].astype(F32)
            g = mine[1, s, :, cols].astype(F32) + theirs[1, s, :, cols].astype(F32)
            sigma = jax.nn.sigmoid(p)
            mine[0, s, :, cols] = (p * sigma).astype(BF16)
            mine[1, s, :, cols] = (g * (sigma * (1.0 + p * (1.0 - sigma)))).astype(BF16)

        v.gl_out[s, 0] = tn(mine[0, s], rank_tokens(COT, s)).astype(BF16)
        v.gr_out[s, 0] = tn(rank_tokens(BWD, s), mine[1, s]).astype(BF16)

        @pl.when((d > 0) & (d + 2 >= S))
        def _():
            for k in range(2):
                grad_z(k, d).start()

        @pl.when(d < FULL)
        def _():
            v.gl_out[s, 1] = tn(mine[0, s], rank_tokens(COT, s, 1 - r)).astype(BF16)
            v.gr_out[s, 1] = tn(rank_tokens(BWD, s, 1 - r), mine[1, s]).astype(BF16)

        @pl.when((d < FULL) & (d > 0))
        def _():
            for k in range(2):
                grad_z(k, d, 1).start()

        @pl.when(d == 0)
        def _():
            for k in range(2):
                for other in range(2):
                    grad_keep(k, other).start()

        @pl.loop(0, width // TILE)
        def _(n):
            cols = at(n, TILE)
            by_owner(v.rs_b, s, cols, nt(mine[1, s], wu[cols, :]))

        by_owner(v.rs_b, s, slice(width, width + share), nt(mine[1, s], rt[s]))
        by_owner(v.rs_b, s, slice(width + share, width + 2 * share), nn(mine[0, s], lt[s]))
        rs_k(0, d).start()

    def fwd_chunk(d):
        s = behind(d)
        pre(2, d).wait()

        @pl.loop(0, units // min(TILE, units))
        def _(n):
            cols = at(n, min(TILE, units))
            p = mine[2, s, :, cols].astype(F32) + theirs[2, s, :, cols].astype(F32)
            mine[2, s, :, cols] = (p * jax.nn.sigmoid(p)).astype(BF16)

        @pl.loop(0, width // TILE)
        def _(n):
            cols = at(n, TILE)
            by_owner(v.rs_f, s, cols, nn(mine[2, s], wd[:, cols]))

        by_owner(v.rs_f, s, slice(width, width + share), nn(mine[2, s], lt[s]))
        rs_k(1, d).start()

    def reduce_core(j, d):
        s = behind(d)
        rs, rk = sums(j)[:2]
        rs_k(j, d).wait()
        rs[s, core] = (rs[s, core].astype(F32) + rk[s].astype(F32)).astype(BF16)
        for g in range(1, Y):
            rs_y(j, d, g).start()

    def reduce_chunk(j, d):
        s = behind(d)
        rs, _, ry, zs, zr = sums(j)
        total = rs[s, core, y].astype(F32)
        for g in range(1, Y):
            rs_y_in(j, d, g).wait_recv()
            total = total + ry[s, y_down(g)].astype(F32)

        @pl.when(d == 0)
        def _():
            zr[0] = total.astype(BF16)

        @pl.when(d == 1)
        def _():
            zs[1] = total.astype(BF16)
            rs_z(j, 1).start()

        @pl.when(d > 1)
        def _():
            rs_z(j, d - 1).wait_recv()
            zs[d] = (total + zr[d - 1].astype(F32)).astype(BF16)
            rs_z(j, d).start()

    def pass_on(d):
        for k in range(2):
            grad_z_in(k, d).wait_recv()
            grad_x(k, d).start()

    def home_sum(j):
        zr = sums(j)[4]
        rs_z(j, S - 1).wait_recv()
        return zr[0].astype(F32) + zr[S - 1].astype(F32)

    def grad_up():
        step = min(TILE, units)

        @pl.loop(0, width // TILE)
        def _(m):
            slot = lax.rem(m, 2)
            put = pltpu.make_async_copy(v.gu_tile.at[slot], gu_o.at[at(m, TILE), :], v.s_gu_put.at[slot])

            @pl.when(m >= 2)
            def _():
                put.wait()

            for n in range(units // step):
                left = tok[BWD, :, :, :, at(m, TILE)].reshape(S * micro, TILE)
                right = mine[1, :, :, n * step : (n + 1) * step].reshape(S * micro, step)
                v.gu_tile[slot, :, n * step : (n + 1) * step] = tn(left, right).astype(BF16)
            put.start()

    def grad_down():
        tall = min(TILE, units)

        @pl.loop(0, units // tall)
        def _(m):
            slot = lax.rem(m, 2)
            put = pltpu.make_async_copy(
                v.gd_tile.at[slot, :tall], gd_o.at[at(m, tall), :], v.s_gd_put.at[slot]
            )

            @pl.when(m >= 2)
            def _():
                put.wait()

            for n in range(width // TILE):
                left = mine[0, :, :, at(m, tall)].reshape(S * micro, tall)
                right = tok[COT, :, :, :, n * TILE : (n + 1) * TILE].reshape(S * micro, TILE)
                v.gd_tile[slot, :tall, n * TILE : (n + 1) * TILE] = tn(left, right).astype(BF16)
            put.start()

    def drain_tiles(sem, tile, out, tall, count):
        for m in range(max(0, count - 2), count):
            pltpu.make_async_copy(
                tile.at[m % 2, :tall], out.at[m * tall : (m + 1) * tall, :], sem.at[m % 2]
            ).wait()

    loads = [
        (xb_h, tok.at[BWD, z, c]),
        (ct_h, tok.at[COT, z, c]),
        (xf_h, tok.at[FWD, z, c]),
        (ul_h, ul),
        (dr_h, dr),
        (wu_h, wu),
        (ur_h.at[my_half, at(z, units)], rt.at[z]),
        (wd_h, wd),
        (dl_h.at[at(z, units), my_half], lt.at[z]),
    ]
    loads = [pltpu.make_async_copy(a, b, v.s_load.at[i]) for i, (a, b) in enumerate(loads)]
    for copy in loads:
        copy.start()
    barrier = pltpu.get_barrier_semaphore()
    pl.semaphore_signal(barrier, inc=1, device_id={ROW: 1 - r}, device_id_type=MESH)
    for e in range(1, C):
        pl.semaphore_signal(barrier, inc=1, device_id={COL: col_up(e)}, device_id_type=MESH)
    for d in range(1, S):
        pl.semaphore_signal(barrier, inc=1, device_id={SECTION: ahead(d)}, device_id_type=MESH)
    for copy in loads[:3]:
        copy.wait()
    pl.semaphore_wait(barrier, S + C - 1)

    spread(BWD, 0)
    spread(COT, 0)
    send(1, False)
    for copy in loads[3:5]:
        copy.wait()
    v.low_part[BWD] = nn(tok[BWD, z, c], ul[...]).astype(BF16)
    v.low_part[COT] = nt(tok[COT, z, c], dr[...]).astype(BF16)
    v.low_part[FWD] = nn(tok[FWD, z, c], ul[...]).astype(BF16)
    low_x().start()
    low_x().wait()
    for t in (BWD, COT):
        for half in range(2):
            cols = pl.ds(half * share, share)
            low[z, c, 2 * t + half] = (v.low_part[t, :, cols].astype(F32) + v.low_in[t, :, cols].astype(F32)).astype(BF16)
    low[z, c, 4] = (v.low_part[FWD, :, my_half].astype(F32) + v.low_in[FWD, :, my_half].astype(F32)).astype(BF16)
    spread(LOW, 0)
    tok_z(LOW, 1).start()
    spread(FWD, 0)
    for copy in loads[5:]:
        copy.wait()
    bwd_partials(0, True)
    fwd_partials(0)
    forward_all(1)

    @pl.loop(0, S)
    def _(i):
        @pl.when(i + 1 < S)
        def _():
            bwd_partials(i + 1, False)

        @pl.when(i + 1 == S)
        def _():
            @pl.loop(1, S)
            def _(d):
                fwd_partials(d)

        @pl.when(i > 0)
        def _():
            reduce_chunk(0, i - 1)

        bwd_chunk(i)
        reduce_core(0, i)

        @pl.when(i == 0)
        def _():
            fwd_chunk(0)
            reduce_core(1, 0)

        @pl.when(i + 2 < S)
        def _():
            forward_all(i + 2)

        @pl.when((i > 0) & (i + 2 < S))
        def _():
            for k in range(2):
                grad_z(k, i).start()

    reduce_chunk(0, S - 1)
    grad_up()

    @pl.loop(1, S)
    def _(i):
        fwd_chunk(i)
        reduce_core(1, i)
        reduce_chunk(1, i - 1)

        @pl.when((i >= FULL) & (i + 1 < S))
        def _():
            pass_on(i)

    reduce_chunk(1, S - 1)

    total = home_sum(0)
    v.rank_out[0] = total[:, width : width + share].astype(BF16)
    v.rank_out[1] = total[:, width + share :].astype(BF16)
    rank_x(0).start()
    grad_norm = total[:, :width] + tok[COT, z, c].astype(F32)
    total = home_sum(1)
    v.rank_out[2] = total[:, width:].astype(BF16)
    rank_x(1).start()
    out = total[:, :width] + tok[FWD, z, c].astype(F32)
    rank_x(0).wait()
    v.rank_all[c, :, :, my_half] = v.rank_out[0:2]
    v.rank_all[c, :, :, other_half] = v.rank_in[0:2]
    for e in range(1, C):
        rank_c(e).start()
    v.hand[0] = (grad_norm + nt(v.rank_all[c, 0], ul[...])).astype(BF16)
    hand(0).start()
    rank_x(1).wait()
    out = out + nn(v.rank_out[2], dr[my_half, :]) + nn(v.rank_in[2], dr[other_half, :])
    v.hand[1] = out.astype(BF16)
    hand(1).start()
    for d in range(S - 1, S):
        pass_on(d)
    for e in range(1, C):
        rank_c_in(e).wait_recv()
    v.gul[...] = tn(tokens(BWD, z), v.rank_all[:, 0].reshape(micro, rank))
    put_up = pltpu.make_async_copy(v.gul, gul_o, v.s_put.at[4])
    put_up.start()
    v.gdr[...] = tn(v.rank_all[:, 1].reshape(micro, rank), tokens(COT, z))
    put_down = pltpu.make_async_copy(v.gdr, gdr_o, v.s_put.at[5])
    put_down.start()
    grad_down()

    for k in range(2):
        for other in range(2):
            grad_keep(k, other).wait()
        for d in range(1, FULL):
            grad_z_in(k, d).wait_recv()
            grad_z_in(k, d, 1).wait_recv()
            grad_z(k, d, 1).wait_send()
            for half in range(2):
                grad_put(k, d, half).start()

    @pl.loop(FULL, S)
    def _(d):
        for k in range(2):
            grad_x(k, d).wait_send()
            grad_x_in(k, d).wait_recv()
            for half in range(2):
                grad_put(k, d, half).start()

    tall = min(TILE, units)
    drain_tiles(v.s_gu_put, v.gu_tile, gu_o, TILE, width // TILE)
    drain_tiles(v.s_gd_put, v.gd_tile, gd_o, tall, units // tall)
    put_up.wait()
    put_down.wait()

    @pl.loop(1, S)
    def _(d):
        for t in range(4):
            tok_z(t, d).wait_send()
        for k in range(2):
            fac(k, d).wait_send()
            grad_z(k, d).wait_send()
            rs_z(k, d).wait_send()

    @pl.loop(0, S)
    def _(d):
        for t in range(4):
            for g in range(Y):
                tok_k(t, d, g).wait_send()
            for g in range(1, Y):
                tok_y(t, d, g).wait_send()
        for j in range(2):
            for g in range(1, Y):
                rs_y(j, d, g).wait_send()

    for e in range(1, C):
        rank_c(e).wait_send()
    for j in range(2):
        hand(j).wait()

    @pl.loop(1, S)
    def _(d):
        for k in range(2):
            for half in range(2):
                grad_put(k, d, half).wait()


def finish_kernel(count, *refs):
    ins, outs, near, wide = refs[:8], refs[8:16], refs[16:24], refs[24:26]
    s_in, s_out = refs[26:]
    pieces = []
    for i in (5, 6, 2, 3, 4, 7, 0, 1):
        parts = count if i in (2, 3, 5, 6) else 1
        tall = ins[i].shape[0] // parts
        for p in range(parts):
            rows = pl.ds(p * tall, tall)
            final = wide[i - 5] if i in (5, 6) else near[i]
            load = pltpu.make_async_copy(ins[i].at[rows], near[i].at[rows], s_in.at[i, p])
            store = pltpu.make_async_copy(final.at[rows], outs[i].at[rows], s_out.at[i, p])
            pieces.append((i, rows, load, store))
    for _, _, load, _ in pieces:
        load.start()
    for i, rows, load, store in pieces:
        load.wait()
        if i in (5, 6):
            wide[i - 5][rows] = near[i][rows].astype(F32)
        store.start()
    for _, _, _, store in pieces:
        store.wait()


def finish(arrays):
    whole, count = pl.BlockSpec(memory_space=pl.ANY), 4
    outs = [jax.ShapeDtypeStruct(a.shape, F32 if i in (5, 6) else a.dtype) for i, a in enumerate(arrays)]
    return pl.pallas_call(
        functools.partial(finish_kernel, count),
        out_shape=outs,
        in_specs=[whole] * len(outs),
        out_specs=[whole] * len(outs),
        scratch_shapes=[pltpu.VMEM(a.shape, a.dtype) for a in arrays]
        + [pltpu.VMEM(outs[i].shape, F32) for i in (5, 6)]
        + [pltpu.SemaphoreType.DMA((8, count))] * 2,
        compiler_params=pltpu.CompilerParams(vmem_limit_bytes=VMEM_BYTES),
    )(*arrays)


def fused(*args):
    S, C = lax.axis_size(SECTION), lax.axis_size(COL)
    own, width = args[0].shape[1:]
    units, rank = args[3].shape[1], args[5].shape[2]
    shapes = scratch_of(S, C, own, width, units, rank)
    outs = [
        ((own, width), BF16),
        ((own, width), BF16),
        ((width, units), BF16),
        ((units, width), BF16),
        ((width, rank), F32),
        ((S * units, rank), BF16),
        ((rank, S * units), BF16),
        ((rank, width), F32),
    ]
    whole = pl.BlockSpec(memory_space=pl.ANY)
    tokens = 3 * S * own * C
    outputs = pl.pallas_call(
        functools.partial(kernel, S, C, list(shapes)),
        out_shape=[jax.ShapeDtypeStruct(*out) for out in outs],
        in_specs=[whole] * len(args),
        out_specs=[whole] * len(outs),
        scratch_shapes=list(shapes.values()),
        compiler_params=pltpu.CompilerParams(
            collective_id=0, has_side_effects=True, vmem_limit_bytes=VMEM_BYTES
        ),
        cost_estimate=pl.CostEstimate(
            flops=6 * tokens * width * units, bytes_accessed=20 * width * units, transcendentals=tokens * units
        ),
    )(*[arg[0] if arg.ndim == 3 else arg for arg in args])
    hand_f, hand_b, grad_up, grad_down, grad_ul, grad_dl, grad_ur, grad_dr = finish(outputs)
    return (
        hand_f[None],
        hand_b[None],
        grad_up,
        grad_down,
        grad_ul[None],
        grad_ur[None],
        grad_dl[None],
        grad_dr[None],
    )


def step(*args):
    S, C, rows = (lax.axis_size(axis) for axis in (SECTION, COL, ROW))
    own, width = args[0].shape[1:]
    units, rank = args[3].shape[1], args[5].shape[2]
    shapes = scratch_of(S, C, own, width, units, rank)
    fits = vmem_need(shapes) <= VMEM_BYTES - (2 << 20)
    even = rows == 2 and S > 2 and C % 2 == 0 and width % TILE == 0 and (units % TILE == 0 or units == 128)
    if fits and even and rank == 256 and own % 16 == 0:
        return fused(*args)
    return local(*args)


def solution(mesh):
    in_specs = (
        P("section", "col", "row"),
        P("section", "col", "row"),
        P("section", "col", "row"),
        P("row", ("col", "section")),
        P(("col", "section"), "row"),
        P("section", "row", None),
        P("section", None, "col"),
        P("section", "col", None),
        P("section", None, "row"),
    )
    out_specs = (
        P("section", "col", "row"),
        P("section", "col", "row"),
        P("row", ("col", "section")),
        P(("col", "section"), "row"),
        P("section", "row", None),
        P("section", None, "col"),
        P("section", "col", None),
        P("section", None, "row"),
    )
    return jax.shard_map(step, mesh=mesh, in_specs=in_specs, out_specs=out_specs, check_vma=False)
```
